32 devices in a mesh: blk: 8 (over z, x), grid: 4 (over y, core).
Axes of the slice: x: 2, y: 2, z: 4, core: 2. Of those that a mesh axis runs over, the one named last changes fastest.
Arguments:
- patches: bfloat16 [4, 1024, 1024], P('grid', 'blk'), may hold values from -6 to 6
- stem_weight: bfloat16 [2, 1024, 768], replicated, may hold values from -0.125 to 0.125
- norm_gain: bfloat16 [768], replicated, may hold values from 0.25 to 1.75
- w_qkv: bfloat16 [768, 1280], replicated, may hold values from -0.21875 to 0.21875
- w_out: bfloat16 [768, 768], replicated, may hold values from -0.21875 to 0.21875
- per_head_scale: float32 [12], replicated, may hold values from 0.05 to 1, as said below
- positions: int32 [1024], replicated, may hold values from 0 to 1023, each once
- d_out: bfloat16 [4, 1024, 768], P('grid', 'blk'), may hold values from -48 to 48
Outputs:
- d_stem_weight: float32 [2, 1024, 768], P(None, None, ('blk', 'grid'))
- d_norm_gain: float32 [768], P(('blk', 'grid'))
- d_w_qkv: float32 [768, 1280], P(('blk', 'grid'))
- d_w_out: float32 [768, 768], P(None, ('blk', 'grid'))
The draws below stay inside these ranges and needn't reach their ends.
Inputs may be any that keep to these rules, and one draw needn't show every extreme that they name: A permutation of the 1024 positions of a band. `per_head_scale`: positive.
All inputs are finite; a program needn't handle non-finite values.
Results may differ from the reference program's by a relative error of at most 0.015.
The reference program's roundings to bfloat16 on the way count: a program that leaves them out, or rounds other values in their place, can miss the bound.
Values may be sent and summed in bfloat16 or wider, within the bound.
A program may use at most 128 MiB of HBM per device.

```python
from functools import partial
import jax
import jax.numpy as jnp
from jax import lax

D = 768
QUERY_HEADS = 12
KEY_VALUE_HEADS = 4
HEAD_SIZE = 64
TR = 8
TC = 16
TOK_DEV = 128
BAND_TOKENS = 1024
PIN = 1024
QD = 768
KD = 256
N_BLK = 8
N_GRID = 4


def draw_per_head_scale(key, part):
    lowest, highest = (0.05, 0.4)
    uniform_draw = jax.random.uniform(key, (QUERY_HEADS,), jnp.float32)
    return jnp.exp(jnp.log(lowest) + uniform_draw * (jnp.log(highest) - jnp.log(lowest)))


def draw_d_out(key, part):
    noise_key = jax.random.fold_in(key, 11)
    order_key = jax.random.fold_in(key, 23)
    owners = N_BLK * N_GRID
    noise = jnp.clip(jax.random.normal(noise_key, (N_GRID, BAND_TOKENS, D), jnp.float32), -6.0, 6.0)
    factor = 8.0
    pairing = jax.random.permutation(order_key, owners).astype(jnp.int32)
    band_index = jnp.arange(N_GRID, dtype=jnp.int32)[:, None]
    block_index = (jnp.arange(BAND_TOKENS, dtype=jnp.int32) // TOK_DEV)[None, :]
    owner = block_index * N_GRID + band_index
    target = jnp.take(pairing, owner.reshape(-1)).reshape(N_GRID, BAND_TOKENS, 1)
    column_block = (jnp.arange(D, dtype=jnp.int32) // (D // owners))[None, None, :]
    heavy = jnp.where(target == column_block, factor, 1.0)
    return jnp.clip(noise * heavy, -48.0, 48.0).astype(jnp.bfloat16)


def block_scale(key, extent, cuts, least, high):
    factor_of, own = 1.0, jax.random.fold_in(key, 6)
    for position, blocks in cuts:
        draws = jnp.exp(jax.random.uniform(jax.random.fold_in(own, position), (blocks,), jnp.float32, least / len(cuts), high / len(cuts)))
        factor_of = factor_of * jnp.repeat(draws, extent[position] // blocks).reshape([-1 if axis == position else 1 for axis in range(len(extent))])
    return factor_of


def scatter_about(own_key, extent, deviation, most, cuts=(), kind=jnp.bfloat16):
    result = jax.random.normal(own_key, extent, jnp.float32) * deviation
    if len(cuts) > 0:
        result = block_scale(own_key, extent, cuts, -0.22, 0.18) * result
    return jnp.clip(result, min=-most, max=most).astype(kind)


def setup_inputs(seed: int = 0) -> dict:
    seeds = jax.random.split(jax.random.key(seed), 9)
    patches = scatter_about(seeds[0], (N_GRID, BAND_TOKENS, PIN), 1.0, 6.0, ((0, 4), (1, 8)))
    stem_weight = scatter_about(seeds[1], (2, PIN, D), (2 * PIN) ** -0.5, 0.125)
    norm_gain = jnp.clip(1.0 + 0.15 * jax.random.normal(seeds[2], (D,), jnp.float32), 0.25, 1.75).astype(jnp.bfloat16)
    w_qkv = scatter_about(seeds[3], (D, QD + 2 * KD), D ** -0.5, 0.21875)
    w_out = scatter_about(seeds[4], (QD, D), QD ** -0.5, 0.21875)
    per_head_scale = draw_per_head_scale(jax.random.fold_in(seeds[8], 71), 0)
    positions = jax.random.permutation(seeds[6], BAND_TOKENS).astype(jnp.int32)
    d_out = draw_d_out(jax.random.fold_in(seeds[8], 71), 0)
    return dict(patches=patches, stem_weight=stem_weight, norm_gain=norm_gain, w_qkv=w_qkv, w_out=w_out, per_head_scale=per_head_scale, positions=positions, d_out=d_out)


def lower(values):
    return lax.optimization_barrier(values.astype(jnp.bfloat16))

def row_norm(values):
    return values * lax.rsqrt(lax.optimization_barrier(jnp.mean(values * values, axis=-1, keepdims=True)) + 1e-05)

def head_norm(values):
    return values * lax.rsqrt(lax.optimization_barrier(jnp.mean(values * values, axis=-1, keepdims=True)) + 1e-06)

def window_blocks(array):
    blocks = array.reshape((N_BLK, TOK_DEV) + array.shape[1:])
    return jnp.concatenate([jnp.roll(blocks, offset, axis=0) for offset in range(4)], axis=1)

def attend_block(per_head_scale, inputs):
    query_tile_block, gradient_block, key_band_window, value_band_window, query_pos, key_pos = inputs
    group_factor = QUERY_HEADS // KEY_VALUE_HEADS
    token_row_count = query_tile_block.shape[0]
    every_key = key_band_window.shape[0]
    visible = (key_pos[None, :] <= query_pos[:, None])[None, None]
    query_wide = query_tile_block.astype(jnp.float32).reshape(token_row_count, KEY_VALUE_HEADS, group_factor, HEAD_SIZE)
    gradient_wide = gradient_block.astype(jnp.float32).reshape(token_row_count, KEY_VALUE_HEADS, group_factor, HEAD_SIZE)
    key_wide = key_band_window.astype(jnp.float32).reshape(every_key, KEY_VALUE_HEADS, HEAD_SIZE)
    value_wide = value_band_window.astype(jnp.float32).reshape(every_key, KEY_VALUE_HEADS, HEAD_SIZE)
    score_scale = per_head_scale.astype(jnp.float32).reshape(KEY_VALUE_HEADS, group_factor)[:, :, None, None]
    attention_scores = jnp.einsum('phiv,chv->hipc', query_wide, key_wide) * score_scale
    attention_scores = jnp.where(visible, attention_scores, -1e+30)
    top = lax.optimization_barrier(jnp.max(attention_scores, axis=-1, keepdims=True))
    weights = jnp.where(visible, jnp.exp(attention_scores - top), 0.0)
    probs = weights / lax.optimization_barrier(jnp.sum(weights, axis=-1, keepdims=True))
    probability_narrow = lower(probs).astype(jnp.float32)
    attention_output = jnp.einsum('ychp,pyu->hycu', probability_narrow, value_wide)
    softmax_delta = jnp.einsum('pyui,pyui->yup', gradient_wide, attention_output)
    probability_gradient = jnp.einsum('phiv,chv->hipc', gradient_wide, value_wide)
    score_gradient = lower(score_scale * probs * (probability_gradient - softmax_delta[..., None])).astype(jnp.float32)
    query_gradient = jnp.einsum('ychp,pyu->hycu', score_gradient, key_wide).reshape(token_row_count, QUERY_HEADS * HEAD_SIZE)
    key_gradient = jnp.einsum('lpma,mlpx->alx', score_gradient, query_wide).reshape(every_key, KEY_VALUE_HEADS * HEAD_SIZE)
    value_gradient = jnp.einsum('lpma,mlpx->alx', probability_narrow, gradient_wide).reshape(every_key, KEY_VALUE_HEADS * HEAD_SIZE)
    return (attention_output.reshape(token_row_count, QUERY_HEADS * HEAD_SIZE), query_gradient, jnp.concatenate([key_gradient, value_gradient], axis=1))

def band_terms(patches, below, stem_weight, norm_gain, w_qkv, w_out, per_head_scale, positions, d_out):
    query_span_width = QUERY_HEADS * HEAD_SIZE
    key_span_width = KEY_VALUE_HEADS * HEAD_SIZE
    stem = jnp.dot(patches, stem_weight[0], preferred_element_type=jnp.float32)
    stem = stem + jnp.dot(below, stem_weight[1], preferred_element_type=jnp.float32)
    token_f = lower(stem).astype(jnp.float32)
    gain_f = norm_gain.astype(jnp.float32)
    normed = row_norm(token_f)
    hidden = lower(normed * gain_f)
    query_key_value = jnp.dot(hidden, w_qkv, preferred_element_type=jnp.float32)
    query = query_key_value[:, :query_span_width].reshape(BAND_TOKENS, QUERY_HEADS, HEAD_SIZE)
    key = query_key_value[:, query_span_width:query_span_width + key_span_width].reshape(BAND_TOKENS, KEY_VALUE_HEADS, HEAD_SIZE)
    query_normalized = lower(head_norm(query)).reshape(BAND_TOKENS, query_span_width)
    key_n = lower(head_norm(key)).reshape(BAND_TOKENS, key_span_width)
    value = lower(query_key_value[:, query_span_width + key_span_width:])
    attention_gradient = lower(jnp.dot(d_out, w_out.T, preferred_element_type=jnp.float32))
    attn_f, query_gradient, dkv = lax.map(partial(attend_block, per_head_scale), (query_normalized.reshape(N_BLK, TOK_DEV, query_span_width), attention_gradient.reshape(N_BLK, TOK_DEV, query_span_width), window_blocks(key_n), window_blocks(value), positions.reshape(N_BLK, TOK_DEV), window_blocks(positions)))
    attention_output = lower(attn_f.reshape(BAND_TOKENS, query_span_width))
    key_value_gradient_sum = jnp.zeros((N_BLK, TOK_DEV, 2 * key_span_width), jnp.float32)
    for offset in range(4):
        key_value_gradient_sum = key_value_gradient_sum + jnp.roll(dkv[:, offset * TOK_DEV:(offset + 1) * TOK_DEV], -offset, axis=0)
    key_value_gradient_sum = key_value_gradient_sum.reshape(BAND_TOKENS, 2 * key_span_width)
    pull_query = jax.vjp(head_norm, query)[1]
    gather_key = jax.vjp(head_norm, key)[1]
    dq_full = pull_query(query_gradient.reshape(BAND_TOKENS, QUERY_HEADS, HEAD_SIZE))[0].reshape(BAND_TOKENS, query_span_width)
    key_gradient_whole = gather_key(key_value_gradient_sum[:, :key_span_width].reshape(BAND_TOKENS, KEY_VALUE_HEADS, HEAD_SIZE))[0].reshape(BAND_TOKENS, key_span_width)
    d_qkv = lower(jnp.concatenate([dq_full, key_gradient_whole, key_value_gradient_sum[:, key_span_width:]], axis=1))
    d_w_qkv = jnp.dot(hidden.T, d_qkv, preferred_element_type=jnp.float32)
    d_w_out = jnp.dot(attention_output.T, d_out, preferred_element_type=jnp.float32)
    d_hidden = jnp.dot(d_qkv, w_qkv.T, preferred_element_type=jnp.float32)
    d_gain = lax.optimization_barrier(jnp.sum(d_hidden * normed, axis=0))
    pull_tokens = jax.vjp(row_norm, token_f)[1]
    d_tokens = lower(d_out.astype(jnp.float32) + pull_tokens(d_hidden * gain_f)[0])
    d_stem = jnp.stack([jnp.dot(patches.T, d_tokens, preferred_element_type=jnp.float32), jnp.dot(below.T, d_tokens, preferred_element_type=jnp.float32)])
    return (d_stem, d_gain, d_w_qkv, d_w_out)

def reference(patches, stem_weight, norm_gain, w_qkv, w_out, per_head_scale, positions, d_out):
    image = patches.reshape(N_GRID, N_BLK, TR, TC, PIN).transpose(0, 2, 1, 3, 4).reshape(N_GRID * TR, N_BLK, TC, PIN)
    shifted = jnp.concatenate([image[1:], jnp.zeros_like(image[:1])], axis=0)
    below = shifted.reshape(N_GRID, TR, N_BLK, TC, PIN).transpose(0, 2, 1, 3, 4).reshape(N_GRID, BAND_TOKENS, PIN)
    totals = band_terms(patches[0], below[0], stem_weight, norm_gain, w_qkv, w_out, per_head_scale, positions, d_out[0])
    for band in range(1, N_GRID):
        terms = band_terms(patches[band], below[band], stem_weight, norm_gain, w_qkv, w_out, per_head_scale, positions, d_out[band])
        totals = jax.tree.map(lambda first, second: first + second, totals, terms)
    return (totals[0], totals[1], totals[2], totals[3])
```

```python
from functools import partial

import jax
import jax.numpy as jnp
from jax import lax
from jax.experimental import pallas as pl
from jax.experimental.pallas import tpu as pltpu
from jax.sharding import PartitionSpec as P

QUERY_HEADS = 12
KEY_VALUE_HEADS = 4
HEAD_SIZE = 64
TC = 16


def shifted(x, axis, by):
    peers = lax.axis_size(axis)
    pairs = [(i, i + by) for i in range(peers) if 0 <= i + by < peers]
    return lax.ppermute(x, axis, pairs)


def passed_along(x, axis, by):
    peers = lax.axis_size(axis)
    return lax.ppermute(x, axis, [(i, (i + by) % peers) for i in range(peers)])


def row_norm(values):
    return values * lax.rsqrt(jnp.mean(values * values, axis=-1, keepdims=True) + 1e-05)


def head_norm(values):
    return values * lax.rsqrt(jnp.mean(values * values, axis=-1, keepdims=True) + 1e-06)


def log2(n):
    return n.bit_length() - 1


def halving_orders(grid_bits, blk_bits):
    y = list(range(grid_bits))
    low = list(range(grid_bits, grid_bits + blk_bits))
    rest = low[1:]
    return [y + rest[:1] + rest[1:] + low[:1], low[:1] + y + rest, rest[:1] + low[:1] + y + rest[1:]]


def chip_partner(bit, grid_bits, own_blk, own_grid):
    if bit < grid_bits:
        step = 2 << bit
        mine = own_grid // step % 2
        return {"blk": own_blk, "grid": own_grid + (1 - 2 * mine) * step}, mine
    step = 1 << (bit - grid_bits)
    mine = own_blk // step % 2
    return {"blk": own_blk + (1 - 2 * mine) * step, "grid": own_grid}, mine


def transposed_dot(a, b):
    return lax.dot_general(a, b, (((0,), (0,)), ((), ())), preferred_element_type=jnp.float32)


def scatter_kernel(nb, grid_bits, orders, widths, tok_ref, hid_ref, out_grad_ref, stem_ref, attn_ref, dqkv_ref, gain_ref, result_ref, *scratch):
    scratch = list(scratch)
    parts = len(widths)
    first = [scratch.pop(0) for _ in range(parts)]
    recv = [[scratch.pop(0) for _ in range(nb)] for _ in range(parts)]
    send = [[None] + [scratch.pop(0) for _ in range(nb - 1)] for _ in range(parts)]
    keep = [[scratch.pop(0) for _ in range(nb - 1)] for _ in range(parts)]
    final, final_recv, send_sem, recv_sem, final_send, final_got = scratch
    own_blk = lax.axis_index("blk")
    own_grid = lax.axis_index("grid")
    core = own_grid % 2
    other_core = {"blk": own_blk, "grid": own_grid + 1 - 2 * core}
    barrier = pltpu.get_barrier_semaphore()
    for bit in range(nb):
        pl.semaphore_signal(barrier, inc=1, device_id=chip_partner(bit, grid_bits, own_blk, own_grid)[0], device_id_type=pl.DeviceIdType.MESH)
    pl.semaphore_signal(barrier, inc=1, device_id=other_core, device_id_type=pl.DeviceIdType.MESH)
    pl.semaphore_wait(barrier, nb + 1)

    def transfer(part, step, source):
        partner, mine = chip_partner(orders[part][step], grid_bits, own_blk, own_grid)
        copy = pltpu.make_async_remote_copy(
            src_ref=source,
            dst_ref=recv[part][step],
            send_sem=send_sem.at[part, step],
            recv_sem=recv_sem.at[part, step],
            device_id=partner,
            device_id_type=pl.DeviceIdType.MESH,
        )
        copy.start()
        return copy

    rows = final.shape[1] * 2
    segments = [
        [(tok_ref, stem_ref, 0, widths[0])],
        [(tok_ref, stem_ref, widths[0], stem_ref.shape[1] - widths[0]), (out_grad_ref, attn_ref, 0, attn_ref.shape[1])],
        [(hid_ref, dqkv_ref, 0, dqkv_ref.shape[1])],
    ]
    copies = [None] * parts
    for part in (2, 1, 0):
        at = 0
        for left, right, start, width in segments[part]:
            product = transposed_dot(left[...], right[:, start : start + width]).astype(jnp.bfloat16)
            first[part][:, :, :, :, at : at + width] = product.reshape(first[part].shape[:4] + (width,))
            at += width
        if part == 2:
            first[part][:, :, :, :, at:] = gain_ref[...].reshape(first[part].shape[:4] + (gain_ref.shape[1],))
        mine = chip_partner(orders[part][0], grid_bits, own_blk, own_grid)[1]
        copies[part] = transfer(part, 0, first[part].at[:, 1 - mine])

    done = [None] * parts
    for step in range(nb):
        for part in (2, 1, 0):
            copies[part].wait()
            held = recv[part][step]
            left_over = [b for b in range(nb) if b not in orders[part][:step]]
            mine = chip_partner(orders[part][step], grid_bits, own_blk, own_grid)[1]
            if step == 0:
                inner = first[part].shape[2]

                def total(i):
                    return first[part][i // inner, mine, i % inner].astype(jnp.float32) + held[i // inner, i % inner].astype(jnp.float32)
            else:
                place = 1 << left_over.index(orders[part][step])

                def total(i):
                    return keep[part][step - 1][i // place * (2 * place) + mine * place + i % place] + held[i].astype(jnp.float32)

            if step == nb - 1:
                done[part] = total(0)
                continue
            left_over.remove(orders[part][step])
            bit = orders[part][step + 1]
            place_next = 1 << left_over.index(bit)
            mine_next = chip_partner(bit, grid_bits, own_blk, own_grid)[1]
            count = 1 << (nb - 1 - step)
            for r in range(count // 2):
                away = r // place_next * (2 * place_next) + (1 - mine_next) * place_next + r % place_next
                send[part][step + 1][r] = total(away).astype(jnp.bfloat16)
            copies[part] = transfer(part, step + 1, send[part][step + 1])
            for r in range(count // 2):
                here = r // place_next * (2 * place_next) + mine_next * place_next + r % place_next
                keep[part][step][here] = total(here)
    at = 0
    half = rows // 2
    for part in range(parts):
        final[0, :, at : at + widths[part]] = done[part][:half]
        final[1, :, at : at + widths[part]] = done[part][half:]
        at += widths[part]
    copy = pltpu.make_async_remote_copy(
        src_ref=final.at[1 - core],
        dst_ref=final_recv,
        send_sem=final_send,
        recv_sem=final_got,
        device_id=other_core,
        device_id_type=pl.DeviceIdType.MESH,
    )
    copy.start()
    result_ref[core] = final[core]
    copy.wait()
    result_ref[1 - core] = final_recv[...]


def scatter_all(tokens_grad, hidden, grad_out, stem_side, attn_side, qkv_side, gain):
    blk_bits, grid_bits = log2(lax.axis_size("blk")), log2(lax.axis_size("grid")) - 1
    nb = blk_bits + grid_bits
    features = tokens_grad.shape[1]
    rows = features >> nb
    gain_tile = jnp.broadcast_to(gain.astype(jnp.bfloat16)[:, None], (features, 128))
    stem_width = stem_side.shape[1]
    widths = [stem_width * 3 // 4, stem_width // 4 + attn_side.shape[1], qkv_side.shape[1] + 128]
    orders = halving_orders(grid_bits, blk_bits)
    firsts, recvs, sends, keeps = [], [], [], []
    for order, width in zip(orders, widths):
        inner = 1 << order[0]
        outer = (1 << nb) // (2 * inner)
        firsts.append(pltpu.VMEM((outer, 2, inner, rows, width), jnp.bfloat16))
        recvs.append(pltpu.VMEM((outer, inner, rows, width), jnp.bfloat16))
        for step in range(1, nb):
            shape = (1 << (nb - 1 - step), rows, width)
            recvs.append(pltpu.VMEM(shape, jnp.bfloat16))
            sends.append(pltpu.VMEM(shape, jnp.bfloat16))
            keeps.append(pltpu.VMEM((1 << (nb - step), rows, width), jnp.float32))
    total = sum(widths)
    return pl.pallas_call(
        partial(scatter_kernel, nb, grid_bits, orders, widths),
        out_shape=jax.ShapeDtypeStruct((2, rows // 2, total), jnp.float32),
        in_specs=[pl.BlockSpec(memory_space=pltpu.VMEM)] * 7,
        out_specs=pl.BlockSpec(memory_space=pltpu.VMEM),
        scratch_shapes=firsts
        + recvs
        + sends
        + keeps
        + [
            pltpu.VMEM((2, rows // 2, total), jnp.float32),
            pltpu.VMEM((rows // 2, total), jnp.float32),
            pltpu.SemaphoreType.DMA((3, nb)),
            pltpu.SemaphoreType.DMA((3, nb)),
            pltpu.SemaphoreType.DMA,
            pltpu.SemaphoreType.DMA,
        ],
        compiler_params=pltpu.CompilerParams(collective_id=0, has_side_effects=True, vmem_limit_bytes=60000000),
    )(tokens_grad, hidden, grad_out, stem_side, attn_side, qkv_side, gain_tile)


def across_cores(x):
    peers = lax.axis_size("grid")
    return lax.ppermute(x, "grid", [(i, i ^ 1) for i in range(peers)])


def halved(x, core):
    half = x.shape[1] // 2
    return lax.dynamic_slice_in_dim(x, core * half, half, 1)


def shards(patches, stem_weight, norm_gain, w_qkv, w_out, per_head_scale, positions, d_out):
    tiles = patches[0]
    grad_out = d_out[0]
    token_rows = tiles.shape[0]
    group_factor = QUERY_HEADS // KEY_VALUE_HEADS
    query_span_width = QUERY_HEADS * HEAD_SIZE
    key_span_width = KEY_VALUE_HEADS * HEAD_SIZE
    arrived = shifted(tiles[:TC], "grid", -1)
    below = jnp.concatenate([tiles[TC:], arrived], axis=0)
    core = lax.axis_index("grid") % 2
    own_plane = jnp.where(core == 0, tiles, below)
    stem_side = jnp.concatenate([own_plane, across_cores(jnp.where(core == 0, below, tiles))], axis=0)
    grad_pair = jnp.concatenate([grad_out, across_cores(grad_out)], axis=0)
    stem = jnp.dot(tiles, stem_weight[0], preferred_element_type=jnp.float32)
    stem = stem + jnp.dot(below, stem_weight[1], preferred_element_type=jnp.float32)
    token_f = lax.optimization_barrier(stem.astype(jnp.bfloat16)).astype(jnp.float32)
    gain_f = norm_gain.astype(jnp.float32)
    normed = row_norm(token_f)
    hidden = (normed * gain_f).astype(jnp.bfloat16)
    query_key_value = jnp.dot(hidden, w_qkv, preferred_element_type=jnp.float32)
    query = query_key_value[:, :query_span_width].reshape(token_rows, QUERY_HEADS, HEAD_SIZE)
    key = query_key_value[:, query_span_width : query_span_width + key_span_width].reshape(
        token_rows, KEY_VALUE_HEADS, HEAD_SIZE
    )
    query_normalized = head_norm(query).astype(jnp.bfloat16)
    key_n = head_norm(key).astype(jnp.bfloat16).reshape(token_rows, key_span_width)
    value = query_key_value[:, query_span_width + key_span_width :].astype(jnp.bfloat16)
    attention_gradient = jnp.dot(grad_out, w_out.T, preferred_element_type=jnp.float32).astype(
        jnp.bfloat16
    )
    kv_own = jnp.concatenate([key_n, value], axis=1)
    blk_count = lax.axis_size("blk")
    own_index = lax.axis_index("blk")
    blocks = [kv_own]
    for offset in range(1, 4):
        blocks.append(passed_along(kv_own, "blk", offset))
    causal_window = jnp.concatenate(blocks, axis=0)
    key_pos = jnp.concatenate(
        [
            lax.dynamic_slice_in_dim(
                positions, (own_index - offset) % blk_count * token_rows, token_rows
            )
            for offset in range(4)
        ]
    )
    query_pos = lax.dynamic_slice_in_dim(positions, own_index * token_rows, token_rows)
    visible = (key_pos[None, :] <= query_pos[:, None])[None]
    every_key = causal_window.shape[0]
    query_cube = query_normalized.reshape(token_rows, KEY_VALUE_HEADS, group_factor, HEAD_SIZE)
    gradient_cube = attention_gradient.reshape(token_rows, KEY_VALUE_HEADS, group_factor, HEAD_SIZE)
    key_cube = causal_window[:, :key_span_width].reshape(every_key, KEY_VALUE_HEADS, HEAD_SIZE)
    value_cube = causal_window[:, key_span_width:].reshape(every_key, KEY_VALUE_HEADS, HEAD_SIZE)
    score_scales = per_head_scale.reshape(KEY_VALUE_HEADS, group_factor)
    prob_list = []
    low_list = []
    attn_list = []
    for query_head_group in range(KEY_VALUE_HEADS):
        scale_col = score_scales[query_head_group][:, None, None]
        attention_scores = (
            jnp.einsum(
                "trd,sd->rts",
                query_cube[:, query_head_group],
                key_cube[:, query_head_group],
                preferred_element_type=jnp.float32,
            )
            * scale_col
        )
        attention_scores = jnp.where(visible, attention_scores, -1e30)
        top = jnp.max(attention_scores, axis=-1, keepdims=True)
        weights = jnp.where(visible, jnp.exp(attention_scores - top), 0.0)
        probs = weights / jnp.sum(weights, axis=-1, keepdims=True)
        probability_narrow = probs.astype(jnp.bfloat16)
        prob_list.append(probs)
        low_list.append(probability_narrow)
        attn_list.append(
            jnp.einsum(
                "rts,sd->trd",
                probability_narrow,
                value_cube[:, query_head_group],
                preferred_element_type=jnp.float32,
            )
        )
    attention_output = (
        jnp.stack(attn_list, axis=1).reshape(token_rows, query_span_width).astype(jnp.bfloat16)
    )
    attn_side = jnp.concatenate(
        [halved(attention_output, core), across_cores(halved(attention_output, 1 - core))], axis=0
    )
    hidden_pair = jnp.concatenate([hidden, across_cores(hidden)], axis=0)
    dquery_list = []
    dkey_list = []
    dvalue_list = []
    for query_head_group in range(KEY_VALUE_HEADS):
        scale_col = score_scales[query_head_group][:, None, None]
        grad_group = gradient_cube[:, query_head_group]
        softmax_delta = jnp.sum(
            grad_group.astype(jnp.float32) * attn_list[query_head_group], axis=-1
        )
        probability_gradient = jnp.einsum(
            "trd,sd->rts",
            grad_group,
            value_cube[:, query_head_group],
            preferred_element_type=jnp.float32,
        )
        score_gradient = (
            scale_col
            * prob_list[query_head_group]
            * (probability_gradient - softmax_delta.T[:, :, None])
        ).astype(jnp.bfloat16)
        dquery_list.append(
            jnp.einsum(
                "rts,sd->trd",
                score_gradient,
                key_cube[:, query_head_group],
                preferred_element_type=jnp.float32,
            )
        )
        dkey_list.append(
            jnp.einsum(
                "rts,trd->sd",
                score_gradient,
                query_cube[:, query_head_group],
                preferred_element_type=jnp.float32,
            )
        )
        dvalue_list.append(
            jnp.einsum(
                "rts,trd->sd",
                low_list[query_head_group],
                grad_group,
                preferred_element_type=jnp.float32,
            )
        )
    query_gradient = jnp.stack(dquery_list, axis=1).reshape(token_rows, QUERY_HEADS, HEAD_SIZE)
    dkey_all = jnp.stack(dkey_list, axis=1).reshape(every_key, key_span_width)
    dvalue_all = jnp.stack(dvalue_list, axis=1).reshape(every_key, key_span_width)
    partial_terms = jnp.concatenate([dkey_all, dvalue_all], axis=1)
    pieces = [partial_terms[offset * token_rows : (offset + 1) * token_rows] for offset in range(4)]
    carried_state = pieces[0]
    for offset in (1, 2, 3):
        carried_state = carried_state + passed_along(pieces[offset], "blk", -offset)
    pull_query = jax.vjp(head_norm, query)[1]
    gather_key = jax.vjp(head_norm, key)[1]
    dq_full = pull_query(query_gradient)[0].reshape(token_rows, query_span_width)
    key_gradient_whole = gather_key(
        carried_state[:, :key_span_width].reshape(token_rows, KEY_VALUE_HEADS, HEAD_SIZE)
    )[0].reshape(token_rows, key_span_width)
    d_qkv = jnp.concatenate(
        [dq_full, key_gradient_whole, carried_state[:, key_span_width:]], axis=1
    ).astype(jnp.bfloat16)
    qkv_side = jnp.concatenate([halved(d_qkv, core), across_cores(halved(d_qkv, 1 - core))], axis=0)
    d_hidden = jnp.dot(d_qkv, w_qkv.T, preferred_element_type=jnp.float32)
    gain_term = jnp.sum(d_hidden * normed, axis=0)
    pull_tokens = jax.vjp(row_norm, token_f)[1]
    d_tokens = (grad_out.astype(jnp.float32) + pull_tokens(d_hidden * gain_f)[0]).astype(
        jnp.bfloat16
    )
    tokens_pair = jnp.concatenate([d_tokens, across_cores(d_tokens)], axis=0)
    chips = blk_count * lax.axis_size("grid") // 2
    if (d_tokens.shape[1] // chips) % 16 == 0:
        parts = scatter_all(tokens_pair, hidden_pair, grad_pair, stem_side, attn_side, qkv_side, gain_term)
        stem_width, attn_width, qkv_width = stem_side.shape[1], attn_side.shape[1], qkv_side.shape[1]
        d_stem_weight = parts[:, :, :stem_width].transpose(0, 2, 1)
        d_w_out = parts[:, :, stem_width : stem_width + attn_width].transpose(0, 2, 1).reshape(2 * attn_width, -1)
        start = stem_width + attn_width
        d_w_qkv = jnp.concatenate([parts[0, :, start : start + qkv_width], parts[1, :, start : start + qkv_width]], axis=1)
        d_norm_gain = parts[0, :, start + qkv_width] + parts[1, :, start + qkv_width]
        return (d_stem_weight, d_norm_gain, d_w_qkv, d_w_out)
    stem_term = jnp.stack(
        [
            jnp.dot(tiles.T, d_tokens, preferred_element_type=jnp.float32),
            jnp.dot(below.T, d_tokens, preferred_element_type=jnp.float32),
        ]
    )
    qkv_term = jnp.dot(hidden.T, d_qkv, preferred_element_type=jnp.float32)
    out_term = jnp.dot(attention_output.T, grad_out, preferred_element_type=jnp.float32)
    d_stem_weight = lax.psum_scatter(stem_term, ("blk", "grid"), scatter_dimension=2, tiled=True)
    d_norm_gain = lax.psum_scatter(gain_term, ("blk", "grid"), scatter_dimension=0, tiled=True)
    d_w_qkv = lax.psum_scatter(qkv_term, ("blk", "grid"), scatter_dimension=0, tiled=True)
    d_w_out = lax.psum_scatter(out_term, ("blk", "grid"), scatter_dimension=1, tiled=True)
    return (d_stem_weight, d_norm_gain, d_w_qkv, d_w_out)


def solution(mesh):
    placed = (P("grid", "blk", None), P(), P(), P(), P(), P(), P(), P("grid", "blk", None))
    return jax.shard_map(
        shards,
        mesh=mesh,
        in_specs=placed,
        out_specs=(
            P(None, None, ("blk", "grid")),
            P(("blk", "grid")),
            P(("blk", "grid"), None),
            P(None, ("blk", "grid")),
        ),
        check_vma=False,
    )
```

```python
from functools import partial

import jax
import jax.numpy as jnp
from jax import lax
from jax.experimental import pallas as pl
from jax.experimental.pallas import tpu as pltpu
from jax.sharding import PartitionSpec as P

QUERY_HEADS = 12
KEY_VALUE_HEADS = 4
HEAD_SIZE = 64
TC = 16


def shifted(x, axis, by):
    peers = lax.axis_size(axis)
    pairs = [(i, i + by) for i in range(peers) if 0 <= i + by < peers]
    return lax.ppermute(x, axis, pairs)


def passed_along(x, axis, by):
    peers = lax.axis_size(axis)
    return lax.ppermute(x, axis, [(i, (i + by) % peers) for i in range(peers)])


def row_norm(values):
    return values * lax.rsqrt(jnp.mean(values * values, axis=-1, keepdims=True) + 1e-05)


def head_norm(values):
    return values * lax.rsqrt(jnp.mean(values * values, axis=-1, keepdims=True) + 1e-06)


def log2(n):
    return n.bit_length() - 1


def halving_orders(grid_bits, blk_bits):
    y = list(range(grid_bits))
    low = list(range(grid_bits, grid_bits + blk_bits))
    rest = low[1:]
    return [y + rest[:1] + rest[1:] + low[:1], low[:1] + y + rest, rest[:1] + low[:1] + y + rest[1:]]


def chip_partner(bit, grid_bits, own_blk, own_grid):
    if bit < grid_bits:
        step = 2 << bit
        mine = own_grid // step % 2
        return {"blk": own_blk, "grid": own_grid + (1 - 2 * mine) * step}, mine
    step = 1 << (bit - grid_bits)
    mine = own_blk // step % 2
    return {"blk": own_blk + (1 - 2 * mine) * step, "grid": own_grid}, mine


def transposed_dot(a, b):
    return lax.dot_general(a, b, (((0,), (0,)), ((), ())), preferred_element_type=jnp.float32)


def rowwise_dot(a, b):
    return lax.dot_general(a, b, (((1,), (1,)), ((), ())), preferred_element_type=jnp.float32)


def plain_dot(a, b):
    return jnp.dot(a, b, preferred_element_type=jnp.float32)


def half_sums(x):
    low = lax.broadcasted_iota(jnp.int32, x.shape, 1) < HEAD_SIZE
    first = jnp.sum(jnp.where(low, x, 0.0), axis=1, keepdims=True)
    second = jnp.sum(jnp.where(low, 0.0, x), axis=1, keepdims=True)
    return jnp.where(low, first, second)


def layer_kernel(plan, *refs):
    nb, grid_bits, orders, widths, offsets = plan
    (scale_ref, tiles_ref, grad_ref, stem_hbm, gain_ref, wqkv_hbm, wout_hbm, pos_ref, result_ref) = refs[:9]
    scratch = list(refs[9:])
    parts = len(widths)
    first = [scratch.pop(0) for _ in range(parts)]
    recv = [[scratch.pop(0) for _ in range(nb)] for _ in range(parts)]
    send = [[None] + [scratch.pop(0) for _ in range(nb - 1)] for _ in range(parts)]
    keep = [[scratch.pop(0) for _ in range(nb - 1)] for _ in range(parts)]
    (final, final_recv, stem_w, wqkv, wout, image, grad_pair, hidden_pair, attn_pair, dqkv_pair, token_pair,
     kv, dkv_out, dkv_own, dkv_in, normed_ref, inv_ref, qk_ref, heads_inv, qn, da, attn, dq, dqkv,
     load_sem, pair_send, pair_got, halo_send, halo_got, kv_send, kv_got, dkv_send, dkv_got, send_sem, recv_sem) = scratch
    tok, width = grad_ref.shape
    halo = image.shape[0] - 2 * tok
    span = kv.shape[2] // 2
    group = QUERY_HEADS // KEY_VALUE_HEADS
    own_blk = lax.axis_index("blk")
    own_grid = lax.axis_index("grid")
    blk_count = lax.axis_size("blk")
    grid_count = lax.axis_size("grid")
    core = own_grid % 2
    other_core = {"blk": own_blk, "grid": own_grid + 1 - 2 * core}
    above = {"blk": own_blk, "grid": (own_grid + grid_count - 1) % grid_count}
    under = {"blk": own_blk, "grid": (own_grid + 1) % grid_count}

    def along(offset):
        return {"blk": (own_blk + offset + blk_count) % blk_count, "grid": own_grid}

    loads = [
        pltpu.make_async_copy(stem_hbm, stem_w, load_sem.at[0]),
        pltpu.make_async_copy(wqkv_hbm, wqkv, load_sem.at[1]),
        pltpu.make_async_copy(wout_hbm, wout, load_sem.at[2]),
    ]
    for load in loads:
        load.start()

    barrier = pltpu.get_barrier_semaphore()
    peers = [chip_partner(bit, grid_bits, own_blk, own_grid)[0] for bit in range(nb)]
    peers += [other_core, above, under] + [along(j) for j in (1, 2, 3, -1, -2, -3)]
    for peer in peers:
        pl.semaphore_signal(barrier, inc=1, device_id=peer, device_id_type=pl.DeviceIdType.MESH)
    pl.semaphore_wait(barrier, len(peers))

    def push(source, target, sems, got, device):
        copy = pltpu.make_async_remote_copy(
            src_ref=source, dst_ref=target, send_sem=sems, recv_sem=got, device_id=device, device_id_type=pl.DeviceIdType.MESH
        )
        copy.start()
        return copy

    def pair(which, source, target):
        return push(source, target, pair_send.at[which], pair_got.at[which], other_core)

    own_rows = pl.ds(pl.multiple_of(core * tok, tok), tok)
    tiles_copy = pair(0, tiles_ref, image.at[own_rows])
    halo_copy = push(tiles_ref.at[:halo], image.at[2 * tok :], halo_send, halo_got, above)
    grad_copy = pair(1, grad_ref, grad_pair.at[core])
    image[own_rows] = tiles_ref[...]
    grad_pair[core] = grad_ref[...]

    loads[0].wait()
    stem = plain_dot(tiles_ref[...], stem_w[0])
    tiles_copy.wait()
    halo_copy.wait()

    @pl.when(own_grid == grid_count - 1)
    def _():
        image[2 * tok :] = jnp.zeros((halo, image.shape[1]), image.dtype)

    below = image[pl.ds(pl.multiple_of(core * tok + halo, halo), tok)]
    stem = stem + plain_dot(below, stem_w[1])
    token_f = stem.astype(jnp.bfloat16).astype(jnp.float32)
    inv = lax.rsqrt(jnp.sum(token_f * token_f, axis=1, keepdims=True) / width + 1e-05)
    normed = token_f * inv
    normed_ref[...] = normed
    inv_ref[...] = jnp.broadcast_to(inv, inv_ref.shape)
    gain_f = gain_ref[...].astype(jnp.float32)
    hidden = (normed * gain_f).astype(jnp.bfloat16)
    hidden_pair[core] = hidden
    hidden_copy = pair(2, hidden_pair.at[core], hidden_pair.at[core])
    loads[1].wait()
    key_start = QUERY_HEADS * HEAD_SIZE
    value_start = key_start + span

    def normalize(x):
        scale = lax.rsqrt(half_sums(x * x) / HEAD_SIZE + 1e-06)
        return scale, (x * scale).astype(jnp.bfloat16)

    keys = plain_dot(hidden, wqkv[:, key_start:])
    for at in range(0, span, 128):
        x = keys[:, at : at + 128]
        heads_inv[:, key_start + at : key_start + at + 128], kv[0, :, at : at + 128] = normalize(x)
    kv[0, :, span:] = keys[:, span:].astype(jnp.bfloat16)
    qk_ref[:, key_start:] = keys[:, :span]
    kv_copies = [push(kv.at[0], kv.at[j], kv_send.at[j], kv_got.at[j], along(j)) for j in (1, 2, 3)]
    queries = plain_dot(hidden, wqkv[:, :key_start])
    qk_ref[:, :key_start] = queries
    for at in range(0, key_start, 128):
        heads_inv[:, at : at + 128], qn[:, at : at + 128] = normalize(queries[:, at : at + 128])
    loads[2].wait()
    da[...] = rowwise_dot(grad_ref[...], wout[...]).astype(jnp.bfloat16)

    query_pos = pos_ref[pl.ds(own_blk, 1), :]
    seen = []
    for j in range(4):
        key_pos = pos_ref[pl.ds((own_blk + blk_count - j) % blk_count, 1), :]
        column = jnp.broadcast_to(key_pos, (tok, tok)).T
        seen.append(column <= query_pos)
    visible = jnp.concatenate([jnp.where(x, 1.0, 0.0) for x in seen], axis=0) > 0.5
    for copy in kv_copies:
        copy.wait()

    for g in range(KEY_VALUE_HEADS):
        lanes = slice(g * HEAD_SIZE, (g + 1) * HEAD_SIZE)
        value_lanes = slice(span + g * HEAD_SIZE, span + (g + 1) * HEAD_SIZE)
        keys_g = kv[:, :, lanes].reshape(4 * tok, HEAD_SIZE)
        values_g = kv[:, :, value_lanes].reshape(4 * tok, HEAD_SIZE)
        heads = [slice((g * group + i) * HEAD_SIZE, (g * group + i + 1) * HEAD_SIZE) for i in range(group)]
        queries_g = jnp.concatenate([qn[:, h] for h in heads], axis=0)
        grads_g = jnp.concatenate([da[:, h] for h in heads], axis=0)
        scores = rowwise_dot(keys_g, queries_g)
        dprobs = rowwise_dot(values_g, grads_g)
        probs, low = [], []
        for i in range(group):
            s = jnp.where(visible, scores[:, i * tok : (i + 1) * tok] * scale_ref[g * group + i], -1e30)
            weights = jnp.where(visible, jnp.exp(s - jnp.max(s, axis=0, keepdims=True)), 0.0)
            p = weights * (1.0 / jnp.sum(weights, axis=0, keepdims=True))
            probs.append(p)
            low.append(p.astype(jnp.bfloat16))
        low_g = jnp.concatenate(low, axis=1)
        attn_t = transposed_dot(values_g, low_g)
        delta = jnp.sum(grads_g.astype(jnp.float32).T * attn_t, axis=0, keepdims=True)
        ds = []
        for i in range(group):
            cols = slice(i * tok, (i + 1) * tok)
            ds.append((scale_ref[g * group + i] * probs[i] * (dprobs[:, cols] - delta[:, cols])).astype(jnp.bfloat16))
        ds_g = jnp.concatenate(ds, axis=1)
        dq_g = transposed_dot(keys_g, ds_g).T
        attn_g = attn_t.T
        for i in range(group):
            attn[:, heads[i]] = attn_g[i * tok : (i + 1) * tok].astype(jnp.bfloat16)
            dq[:, heads[i]] = dq_g[i * tok : (i + 1) * tok]
        dkeys = plain_dot(ds_g, queries_g).reshape(4, tok, HEAD_SIZE)
        dvalues = plain_dot(low_g, grads_g).reshape(4, tok, HEAD_SIZE)
        dkv_own[:, lanes] = dkeys[0]
        dkv_own[:, value_lanes] = dvalues[0]
        for j in (1, 2, 3):
            dkv_out[j - 1, :, lanes] = dkeys[j].astype(jnp.bfloat16)
            dkv_out[j - 1, :, value_lanes] = dvalues[j].astype(jnp.bfloat16)
    dkv_copies = [push(dkv_out.at[j - 1], dkv_in.at[j - 1], dkv_send.at[j - 1], dkv_got.at[j - 1], along(-j)) for j in (3, 2, 1)]
    half_attn = attn.shape[1] // 2
    attn_copy = pair(3, attn.at[:, pl.ds(pl.multiple_of((1 - core) * half_attn, 128), half_attn)], attn_pair.at[core])
    attn_pair[core] = attn[:, pl.ds(pl.multiple_of(core * half_attn, 128), half_attn)]

    def pull(at, g):
        scale = heads_inv[:, at : at + 128]
        x = qk_ref[:, at : at + 128] * scale
        return (scale * (g - x * (half_sums(g * x) / HEAD_SIZE))).astype(jnp.bfloat16)

    for at in range(0, key_start, 128):
        dqkv[:, at : at + 128] = pull(at, dq[:, at : at + 128])

    copies = [None] * parts
    steps = [0] * parts
    done = [None] * parts

    def transfer(part, source):
        partner = chip_partner(orders[part][steps[part]], grid_bits, own_blk, own_grid)[0]
        copies[part] = push(source, recv[part][steps[part]], send_sem.at[part, steps[part]], recv_sem.at[part, steps[part]], partner)

    def begin(members, left, right, extra=None):
        product = transposed_dot(left.reshape(2 * tok, width), right).astype(jnp.bfloat16)
        if extra is not None:
            product = jnp.concatenate([product, extra], axis=1)
        at = 0
        for part in members:
            first[part][...] = product[:, at : at + widths[part]].reshape(first[part].shape)
            at += widths[part]
            mine = chip_partner(orders[part][0], grid_bits, own_blk, own_grid)[1]
            transfer(part, first[part].at[:, 1 - mine])

    def advance(part):
        step = steps[part]
        order = orders[part]
        copies[part].wait()
        held = recv[part][step]
        mine = chip_partner(order[step], grid_bits, own_blk, own_grid)[1]
        left_over = [b for b in range(nb) if b not in order[:step]]
        inner = first[part].shape[2]

        def total(i):
            if step == 0:
                return first[part][i // inner, mine, i % inner].astype(jnp.float32) + held[i // inner, i % inner].astype(jnp.float32)
            return keep[part][step - 1][i] + held[i].astype(jnp.float32)

        steps[part] = step + 1
        if step == nb - 1:
            value = total(0)
            half = value.shape[0] // 2
            final[0, :, offsets[part] : offsets[part] + widths[part]] = value[:half]
            final[1, :, offsets[part] : offsets[part] + widths[part]] = value[half:]
            return
        left_over.remove(order[step])
        place_next = 1 << left_over.index(order[step + 1])
        mine_next = chip_partner(order[step + 1], grid_bits, own_blk, own_grid)[1]
        count = 1 << (nb - 2 - step)
        for r in range(count):
            away = r // place_next * (2 * place_next) + (1 - mine_next) * place_next + r % place_next
            send[part][step + 1][r] = total(away).astype(jnp.bfloat16)
        transfer(part, send[part][step + 1])
        for r in range(count):
            here = r // place_next * (2 * place_next) + mine_next * place_next + r % place_next
            keep[part][step][r] = total(here)

    attn_parts, qkv_parts, stem_parts = (0, 1, 2), (3, 4, 5), (6, 7, 8)
    attn_copy.wait()
    grad_copy.wait()
    begin(attn_parts, grad_pair[...], attn_pair[...].reshape(2 * tok, half_attn))

    for copy in dkv_copies:
        copy.wait()
    total_kv = dkv_own[...]
    for j in range(3):
        total_kv = total_kv + dkv_in[j].astype(jnp.float32)
    for at in range(0, span, 128):
        dqkv[:, key_start + at : key_start + at + 128] = pull(key_start + at, total_kv[:, at : at + 128])
    dqkv[:, value_start:] = total_kv[:, span:].astype(jnp.bfloat16)
    half_qkv = dqkv.shape[1] // 2
    dqkv_copy = pair(4, dqkv.at[:, pl.ds(pl.multiple_of((1 - core) * half_qkv, 128), half_qkv)], dqkv_pair.at[core])
    dqkv_pair[core] = dqkv[:, pl.ds(pl.multiple_of(core * half_qkv, 128), half_qkv)]
    d_hidden = rowwise_dot(dqkv[...], wqkv[...])
    normed = normed_ref[...]
    flow = d_hidden * gain_f
    inner_mean = jnp.sum(flow * normed, axis=1, keepdims=True) / width
    d_tokens = grad_ref[...].astype(jnp.float32) + inv_ref[:, :1] * (flow - normed * inner_mean)
    token_pair[core] = d_tokens.astype(jnp.bfloat16)
    token_copy = pair(5, token_pair.at[core], token_pair.at[core])
    gain_term = jnp.sum(d_hidden * normed, axis=0, keepdims=True)
    gain_tile = jnp.broadcast_to(gain_term, (128, width)).T.astype(jnp.bfloat16)
    hidden_copy.wait()
    dqkv_copy.wait()
    begin(qkv_parts, hidden_pair[...], dqkv_pair[...].reshape(2 * tok, half_qkv))
    token_copy.wait()
    begin(stem_parts, token_pair[...], image[pl.ds(pl.multiple_of(core * halo, halo), 2 * tok)], gain_tile)
    for _ in range(nb):
        for part in range(parts):
            advance(part)
    copy = pair(6, final.at[1 - core], final_recv)
    result_ref[core] = final[core]
    copy.wait()
    result_ref[1 - core] = final_recv[...]


def whole_layer(tiles, grad_out, stem_weight, norm_gain, w_qkv, w_out, per_head_scale, positions):
    blk_bits, grid_bits = log2(lax.axis_size("blk")), log2(lax.axis_size("grid")) - 1
    nb = blk_bits + grid_bits
    tok, width = grad_out.shape
    pin = tiles.shape[1]
    qd, span = QUERY_HEADS * HEAD_SIZE, KEY_VALUE_HEADS * HEAD_SIZE
    rows = width >> nb
    half_qkv = w_qkv.shape[1] // 2
    part_widths = []
    for amount in (qd // 2, half_qkv, pin + 128):
        piece = (amount // 3 + 127) // 128 * 128
        part_widths += [piece, piece, amount - 2 * piece]
    offsets = [sum(part_widths[:i]) for i in range(9)]
    orders = halving_orders(grid_bits, blk_bits) * 3
    firsts, recvs, sends, keeps = [], [], [], []
    for order, w in zip(orders, part_widths):
        inner = 1 << order[0]
        outer = (1 << nb) // (2 * inner)
        firsts.append(pltpu.VMEM((outer, 2, inner, rows, w), jnp.bfloat16))
        recvs.append(pltpu.VMEM((outer, inner, rows, w), jnp.bfloat16))
        for step in range(1, nb):
            shape = (1 << (nb - 1 - step), rows, w)
            recvs.append(pltpu.VMEM(shape, jnp.bfloat16))
            sends.append(pltpu.VMEM(shape, jnp.bfloat16))
            keeps.append(pltpu.VMEM(shape, jnp.float32))
    total = sum(part_widths)
    bf, f32 = jnp.bfloat16, jnp.float32
    buffers = [
        ((2, rows // 2, total), f32),
        ((rows // 2, total), f32),
        (stem_weight.shape, bf),
        (w_qkv.shape, bf),
        (w_out.shape, bf),
        ((2 * tok + TC, pin), bf),
        ((2, tok, width), bf),
        ((2, tok, width), bf),
        ((2, tok, qd // 2), bf),
        ((2, tok, half_qkv), bf),
        ((2, tok, width), bf),
        ((4, tok, 2 * span), bf),
        ((3, tok, 2 * span), bf),
        ((tok, 2 * span), f32),
        ((3, tok, 2 * span), bf),
        ((tok, width), f32),
        ((tok, 128), f32),
        ((tok, qd + span), f32),
        ((tok, qd + span), f32),
        ((tok, qd), bf),
        ((tok, qd), bf),
        ((tok, qd), bf),
        ((tok, qd), f32),
        ((tok, w_qkv.shape[1]), bf),
    ]
    dma = pltpu.SemaphoreType.DMA
    vmem = pl.BlockSpec(memory_space=pltpu.VMEM)
    hbm = pl.BlockSpec(memory_space=pl.ANY)
    return part_widths, pl.pallas_call(
        partial(layer_kernel, (nb, grid_bits, orders, part_widths, offsets)),
        out_shape=jax.ShapeDtypeStruct((2, rows // 2, total), f32),
        in_specs=[pl.BlockSpec(memory_space=pltpu.SMEM), vmem, vmem, hbm, vmem, hbm, hbm, vmem],
        out_specs=vmem,
        scratch_shapes=firsts
        + recvs
        + sends
        + keeps
        + [pltpu.VMEM(shape, kind) for shape, kind in buffers]
        + [dma((3,)), dma((7,)), dma((7,)), dma, dma, dma((4,)), dma((4,)), dma((3,)), dma((3,)), dma((9, nb)), dma((9, nb))],
        compiler_params=pltpu.CompilerParams(collective_id=0, has_side_effects=True, vmem_limit_bytes=63000000),
    )(per_head_scale, tiles, grad_out, stem_weight, norm_gain[None], w_qkv, w_out, positions.reshape(-1, tok))


def shards(patches, stem_weight, norm_gain, w_qkv, w_out, per_head_scale, positions, d_out):
    tiles = patches[0]
    grad_out = d_out[0]
    chips = lax.axis_size("blk") * lax.axis_size("grid") // 2
    if (grad_out.shape[1] // chips) % 16 == 0:
        widths, parts = whole_layer(tiles, grad_out, stem_weight, norm_gain, w_qkv, w_out, per_head_scale, positions)
        attn_end = sum(widths[:3])
        qkv_end = sum(widths[:6])
        stem_end = qkv_end + tiles.shape[1]
        return (
            parts[:, :, qkv_end:stem_end].transpose(0, 2, 1),
            parts[0, :, stem_end] + parts[1, :, stem_end],
            jnp.concatenate([parts[0, :, attn_end:qkv_end], parts[1, :, attn_end:qkv_end]], axis=1),
            parts[:, :, :attn_end].transpose(0, 2, 1).reshape(2 * attn_end, -1),
        )
    token_rows = tiles.shape[0]
    group_factor = QUERY_HEADS // KEY_VALUE_HEADS
    query_span_width = QUERY_HEADS * HEAD_SIZE
    key_span_width = KEY_VALUE_HEADS * HEAD_SIZE
    arrived = shifted(tiles[:TC], "grid", -1)
    below = jnp.concatenate([tiles[TC:], arrived], axis=0)
    stem = jnp.dot(tiles, stem_weight[0], preferred_element_type=jnp.float32)
    stem = stem + jnp.dot(below, stem_weight[1], preferred_element_type=jnp.float32)
    token_f = lax.optimization_barrier(stem.astype(jnp.bfloat16)).astype(jnp.float32)
    gain_f = norm_gain.astype(jnp.float32)
    normed = row_norm(token_f)
    hidden = (normed * gain_f).astype(jnp.bfloat16)
    query_key_value = jnp.dot(hidden, w_qkv, preferred_element_type=jnp.float32)
    query = query_key_value[:, :query_span_width].reshape(token_rows, QUERY_HEADS, HEAD_SIZE)
    key = query_key_value[:, query_span_width : query_span_width + key_span_width].reshape(
        token_rows, KEY_VALUE_HEADS, HEAD_SIZE
    )
    query_normalized = head_norm(query).astype(jnp.bfloat16)
    key_n = head_norm(key).astype(jnp.bfloat16).reshape(token_rows, key_span_width)
    value = query_key_value[:, query_span_width + key_span_width :].astype(jnp.bfloat16)
    attention_gradient = jnp.dot(grad_out, w_out.T, preferred_element_type=jnp.float32).astype(
        jnp.bfloat16
    )
    kv_own = jnp.concatenate([key_n, value], axis=1)
    blk_count = lax.axis_size("blk")
    own_index = lax.axis_index("blk")
    blocks = [kv_own]
    for offset in range(1, 4):
        blocks.append(passed_along(kv_own, "blk", offset))
    causal_window = jnp.concatenate(blocks, axis=0)
    key_pos = jnp.concatenate(
        [
            lax.dynamic_slice_in_dim(
                positions, (own_index - offset) % blk_count * token_rows, token_rows
            )
            for offset in range(4)
        ]
    )
    query_pos = lax.dynamic_slice_in_dim(positions, own_index * token_rows, token_rows)
    visible = (key_pos[None, :] <= query_pos[:, None])[None]
    every_key = causal_window.shape[0]
    query_cube = query_normalized.reshape(token_rows, KEY_VALUE_HEADS, group_factor, HEAD_SIZE)
    gradient_cube = attention_gradient.reshape(token_rows, KEY_VALUE_HEADS, group_factor, HEAD_SIZE)
    key_cube = causal_window[:, :key_span_width].reshape(every_key, KEY_VALUE_HEADS, HEAD_SIZE)
    value_cube = causal_window[:, key_span_width:].reshape(every_key, KEY_VALUE_HEADS, HEAD_SIZE)
    score_scales = per_head_scale.reshape(KEY_VALUE_HEADS, group_factor)
    prob_list = []
    low_list = []
    attn_list = []
    for query_head_group in range(KEY_VALUE_HEADS):
        scale_col = score_scales[query_head_group][:, None, None]
        attention_scores = (
            jnp.einsum(
                "trd,sd->rts",
                query_cube[:, query_head_group],
                key_cube[:, query_head_group],
                preferred_element_type=jnp.float32,
            )
            * scale_col
        )
        attention_scores = jnp.where(visible, attention_scores, -1e30)
        top = jnp.max(attention_scores, axis=-1, keepdims=True)
        weights = jnp.where(visible, jnp.exp(attention_scores - top), 0.0)
        probs = weights / jnp.sum(weights, axis=-1, keepdims=True)
        probability_narrow = probs.astype(jnp.bfloat16)
        prob_list.append(probs)
        low_list.append(probability_narrow)
        attn_list.append(
            jnp.einsum(
                "rts,sd->trd",
                probability_narrow,
                value_cube[:, query_head_group],
                preferred_element_type=jnp.float32,
            )
        )
    attention_output = (
        jnp.stack(attn_list, axis=1).reshape(token_rows, query_span_width).astype(jnp.bfloat16)
    )
    dquery_list = []
    dkey_list = []
    dvalue_list = []
    for query_head_group in range(KEY_VALUE_HEADS):
        scale_col = score_scales[query_head_group][:, None, None]
        grad_group = gradient_cube[:, query_head_group]
        softmax_delta = jnp.sum(
            grad_group.astype(jnp.float32) * attn_list[query_head_group], axis=-1
        )
        probability_gradient = jnp.einsum(
            "trd,sd->rts",
            grad_group,
            value_cube[:, query_head_group],
            preferred_element_type=jnp.float32,
        )
        score_gradient = (
            scale_col
            * prob_list[query_head_group]
            * (probability_gradient - softmax_delta.T[:, :, None])
        ).astype(jnp.bfloat16)
        dquery_list.append(
            jnp.einsum(
                "rts,sd->trd",
                score_gradient,
                key_cube[:, query_head_group],
                preferred_element_type=jnp.float32,
            )
        )
        dkey_list.append(
            jnp.einsum(
                "rts,trd->sd",
                score_gradient,
                query_cube[:, query_head_group],
                preferred_element_type=jnp.float32,
            )
        )
        dvalue_list.append(
            jnp.einsum(
                "rts,trd->sd",
                low_list[query_head_group],
                grad_group,
                preferred_element_type=jnp.float32,
            )
        )
    query_gradient = jnp.stack(dquery_list, axis=1).reshape(token_rows, QUERY_HEADS, HEAD_SIZE)
    dkey_all = jnp.stack(dkey_list, axis=1).reshape(every_key, key_span_width)
    dvalue_all = jnp.stack(dvalue_list, axis=1).reshape(every_key, key_span_width)
    partial_terms = jnp.concatenate([dkey_all, dvalue_all], axis=1)
    pieces = [partial_terms[offset * token_rows : (offset + 1) * token_rows] for offset in range(4)]
    carried_state = pieces[0]
    for offset in (1, 2, 3):
        carried_state = carried_state + passed_along(pieces[offset], "blk", -offset)
    pull_query = jax.vjp(head_norm, query)[1]
    gather_key = jax.vjp(head_norm, key)[1]
    dq_full = pull_query(query_gradient)[0].reshape(token_rows, query_span_width)
    key_gradient_whole = gather_key(
        carried_state[:, :key_span_width].reshape(token_rows, KEY_VALUE_HEADS, HEAD_SIZE)
    )[0].reshape(token_rows, key_span_width)
    d_qkv = jnp.concatenate(
        [dq_full, key_gradient_whole, carried_state[:, key_span_width:]], axis=1
    ).astype(jnp.bfloat16)
    d_hidden = jnp.dot(d_qkv, w_qkv.T, preferred_element_type=jnp.float32)
    gain_term = jnp.sum(d_hidden * normed, axis=0)
    pull_tokens = jax.vjp(row_norm, token_f)[1]
    d_tokens = (grad_out.astype(jnp.float32) + pull_tokens(d_hidden * gain_f)[0]).astype(
        jnp.bfloat16
    )
    stem_term = jnp.stack(
        [
            jnp.dot(tiles.T, d_tokens, preferred_element_type=jnp.float32),
            jnp.dot(below.T, d_tokens, preferred_element_type=jnp.float32),
        ]
    )
    qkv_term = jnp.dot(hidden.T, d_qkv, preferred_element_type=jnp.float32)
    out_term = jnp.dot(attention_output.T, grad_out, preferred_element_type=jnp.float32)
    d_stem_weight = lax.psum_scatter(stem_term, ("blk", "grid"), scatter_dimension=2, tiled=True)
    d_norm_gain = lax.psum_scatter(gain_term, ("blk", "grid"), scatter_dimension=0, tiled=True)
    d_w_qkv = lax.psum_scatter(qkv_term, ("blk", "grid"), scatter_dimension=0, tiled=True)
    d_w_out = lax.psum_scatter(out_term, ("blk", "grid"), scatter_dimension=1, tiled=True)
    return (d_stem_weight, d_norm_gain, d_w_qkv, d_w_out)


def solution(mesh):
    placed = (P("grid", "blk", None), P(), P(), P(), P(), P(), P(), P("grid", "blk", None))
    return jax.shard_map(
        shards,
        mesh=mesh,
        in_specs=placed,
        out_specs=(
            P(None, None, ("blk", "grid")),
            P(("blk", "grid")),
            P(("blk", "grid"), None),
            P(None, ("blk", "grid")),
        ),
        check_vma=False,
    )
```

```python
from functools import partial

import jax
import jax.numpy as jnp
from jax import lax
from jax.experimental import pallas as pl
from jax.experimental.pallas import tpu as pltpu
from jax.sharding import PartitionSpec as P

QUERY_HEADS = 12
KEY_VALUE_HEADS = 4
HEAD_SIZE = 64
TC = 16


def shifted(x, axis, by):
    peers = lax.axis_size(axis)
    pairs = [(i, i + by) for i in range(peers) if 0 <= i + by < peers]
    return lax.ppermute(x, axis, pairs)


def passed_along(x, axis, by):
    peers = lax.axis_size(axis)
    return lax.ppermute(x, axis, [(i, (i + by) % peers) for i in range(peers)])


def row_norm(values):
    return values * lax.rsqrt(jnp.mean(values * values, axis=-1, keepdims=True) + 1e-05)


def head_norm(values):
    return values * lax.rsqrt(jnp.mean(values * values, axis=-1, keepdims=True) + 1e-06)


def log2(n):
    return n.bit_length() - 1


def halving_orders(grid_bits, blk_bits):
    y = list(range(grid_bits))
    low = list(range(grid_bits, grid_bits + blk_bits))
    rest = low[1:]
    return [y + rest[:1] + rest[1:] + low[:1], low[:1] + y + rest, rest[:1] + low[:1] + y + rest[1:]]


def chip_partner(bit, grid_bits, own_blk, own_grid):
    if bit < grid_bits:
        step = 2 << bit
        mine = own_grid // step % 2
        return {"blk": own_blk, "grid": own_grid + (1 - 2 * mine) * step}, mine
    step = 1 << (bit - grid_bits)
    mine = own_blk // step % 2
    return {"blk": own_blk + (1 - 2 * mine) * step, "grid": own_grid}, mine


def transposed_dot(a, b):
    return lax.dot_general(a, b, (((0,), (0,)), ((), ())), preferred_element_type=jnp.float32)


def rowwise_dot(a, b):
    return lax.dot_general(a, b, (((1,), (1,)), ((), ())), preferred_element_type=jnp.float32)


def plain_dot(a, b):
    return jnp.dot(a, b, preferred_element_type=jnp.float32)


def half_sums(x):
    low = lax.broadcasted_iota(jnp.int32, x.shape, 1) < HEAD_SIZE
    first = jnp.sum(jnp.where(low, x, 0.0), axis=1, keepdims=True)
    second = jnp.sum(jnp.where(low, 0.0, x), axis=1, keepdims=True)
    return jnp.where(low, first, second)


def layer_kernel(plan, *refs):
    nb, grid_bits, orders, widths, offsets = plan
    (scale_ref, tiles_ref, grad_ref, stem_hbm, gain_ref, wqkv_hbm, wout_hbm, pos_ref, stem_out, gain_out, qkv_out, out_out) = refs[:12]
    scratch = list(refs[12:])
    parts = len(widths)
    first = [scratch.pop(0) for _ in range(parts)]
    recv = [[scratch.pop(0) for _ in range(nb)] for _ in range(parts)]
    send = [[None] + [scratch.pop(0) for _ in range(nb - 1)] for _ in range(parts)]
    keep = [[scratch.pop(0) for _ in range(nb - 1)] for _ in range(parts)]
    (final, final_recv, stem_w, wqkv, wout, image, grad_pair, hidden_pair, attn_pair, dqkv_pair, token_pair,
     kv, dkv_out, dkv_own, dkv_in, normed_ref, inv_ref, qk_ref, heads_inv, qn, da, attn, dq, dqkv,
     load_sem, pair_send, pair_got, halo_send, halo_got, kv_send, kv_got, dkv_send, dkv_got, send_sem, recv_sem) = scratch
    tok, width = grad_ref.shape
    halo = image.shape[0] - 2 * tok
    span = kv.shape[0] * 128
    group = QUERY_HEADS // KEY_VALUE_HEADS
    own_blk = lax.axis_index("blk")
    own_grid = lax.axis_index("grid")
    blk_count = lax.axis_size("blk")
    grid_count = lax.axis_size("grid")
    core = own_grid % 2
    other_core = {"blk": own_blk, "grid": own_grid + 1 - 2 * core}
    above = {"blk": own_blk, "grid": (own_grid + grid_count - 1) % grid_count}
    under = {"blk": own_blk, "grid": (own_grid + 1) % grid_count}

    def along(offset):
        return {"blk": (own_blk + offset + blk_count) % blk_count, "grid": own_grid}

    loads = [
        pltpu.make_async_copy(stem_hbm, stem_w, load_sem.at[0]),
        pltpu.make_async_copy(wqkv_hbm, wqkv, load_sem.at[1]),
        pltpu.make_async_copy(wout_hbm, wout, load_sem.at[2]),
    ]
    for load in loads:
        load.start()

    barrier = pltpu.get_barrier_semaphore()
    peers = [chip_partner(bit, grid_bits, own_blk, own_grid)[0] for bit in range(nb)]
    peers += [other_core, above, under] + [along(j) for j in (1, 2, 3, -1, -2, -3)]
    for peer in peers:
        pl.semaphore_signal(barrier, inc=1, device_id=peer, device_id_type=pl.DeviceIdType.MESH)
    pl.semaphore_wait(barrier, len(peers))

    def push(source, target, sems, got, device):
        copy = pltpu.make_async_remote_copy(
            src_ref=source, dst_ref=target, send_sem=sems, recv_sem=got, device_id=device, device_id_type=pl.DeviceIdType.MESH
        )
        copy.start()
        return copy

    def pair(which, source, target):
        return push(source, target, pair_send.at[which], pair_got.at[which], other_core)

    own_rows = pl.ds(pl.multiple_of(core * tok, tok), tok)
    halo_copy = push(tiles_ref.at[:halo], image.at[2 * tok :], halo_send, halo_got, above)

    loads[0].wait()
    stem = plain_dot(tiles_ref[...], stem_w[0])
    halo_copy.wait()

    @pl.when(own_grid == grid_count - 1)
    def _():
        image[2 * tok :] = jnp.zeros((halo, image.shape[1]), image.dtype)

    below = jnp.concatenate([tiles_ref[halo:], image[2 * tok :]], axis=0)
    stem = stem + plain_dot(below, stem_w[1])
    token_f = stem.astype(jnp.bfloat16).astype(jnp.float32)
    inv = lax.rsqrt(jnp.sum(token_f * token_f, axis=1, keepdims=True) / width + 1e-05)
    normed = token_f * inv
    normed_ref[...] = normed
    inv_ref[...] = jnp.broadcast_to(inv, inv_ref.shape)
    gain_f = gain_ref[...].astype(jnp.float32).reshape(1, width)
    hidden = (normed * gain_f).astype(jnp.bfloat16)
    hidden_pair[core] = hidden
    loads[1].wait()
    key_start = QUERY_HEADS * HEAD_SIZE
    value_start = key_start + span

    def normalize(x):
        scale = lax.rsqrt(half_sums(x * x) / HEAD_SIZE + 1e-06)
        return scale, (x * scale).astype(jnp.bfloat16)

    keys = plain_dot(hidden, wqkv[:, key_start:])
    kv_copies = []
    for u in range(span // 128):
        at = u * 128
        heads_inv[:, key_start + at : key_start + at + 128], kv[u, 0, :, :128] = normalize(keys[:, at : at + 128])
        kv[u, 0, :, 128:] = keys[:, span + at : span + at + 128].astype(jnp.bfloat16)
        kv_copies.append([push(kv.at[u, 0], kv.at[u, j], kv_send.at[u, j], kv_got.at[u, j], along(j)) for j in (3, 2, 1)])
    qk_ref[:, key_start:] = keys[:, :span]
    tiles_copy = pair(0, tiles_ref, image.at[own_rows])
    grad_copy = pair(1, grad_ref, grad_pair.at[core])
    hidden_copy = pair(2, hidden_pair.at[core], hidden_pair.at[core])
    image[own_rows] = tiles_ref[...]
    grad_pair[core] = grad_ref[...]
    queries = plain_dot(hidden, wqkv[:, :key_start])
    qk_ref[:, :key_start] = queries
    for at in range(0, key_start, 128):
        heads_inv[:, at : at + 128], qn[:, at : at + 128] = normalize(queries[:, at : at + 128])
    loads[2].wait()
    da[...] = rowwise_dot(grad_ref[...], wout[...]).astype(jnp.bfloat16)

    query_pos = pos_ref[pl.ds(own_blk, 1), :]
    seen = []
    for j in range(4):
        key_pos = pos_ref[pl.ds((own_blk + blk_count - j) % blk_count, 1), :]
        column = jnp.broadcast_to(key_pos, (tok, tok)).T
        seen.append(column <= query_pos)
    visible = jnp.concatenate([jnp.where(x, 1.0, 0.0) for x in seen], axis=0) > 0.5
    dkv_copies = []
    for g in range(KEY_VALUE_HEADS):
        u, low_lane = g // 2, g % 2 * HEAD_SIZE
        lanes = slice(low_lane, low_lane + HEAD_SIZE)
        value_lanes = slice(128 + low_lane, 128 + low_lane + HEAD_SIZE)
        if g % 2 == 0:
            for copy in kv_copies[u]:
                copy.wait()
        keys_g = kv[u, :, :, lanes].reshape(4 * tok, HEAD_SIZE)
        values_g = kv[u, :, :, value_lanes].reshape(4 * tok, HEAD_SIZE)
        heads = [slice((g * group + i) * HEAD_SIZE, (g * group + i + 1) * HEAD_SIZE) for i in range(group)]
        queries_g = jnp.concatenate([qn[:, h] for h in heads], axis=0)
        grads_g = jnp.concatenate([da[:, h] for h in heads], axis=0)
        scores = rowwise_dot(keys_g, queries_g)
        dprobs = rowwise_dot(values_g, grads_g)
        probs, low = [], []
        for i in range(group):
            s = jnp.where(visible, scores[:, i * tok : (i + 1) * tok] * scale_ref[g * group + i], -1e30)
            weights = jnp.where(visible, jnp.exp(s - jnp.max(s, axis=0, keepdims=True)), 0.0)
            p = weights * (1.0 / jnp.sum(weights, axis=0, keepdims=True))
            probs.append(p)
            low.append(p.astype(jnp.bfloat16))
        low_g = jnp.concatenate(low, axis=1)
        attn_t = transposed_dot(values_g, low_g)
        delta = jnp.sum(grads_g.astype(jnp.float32).T * attn_t, axis=0, keepdims=True)
        ds = []
        for i in range(group):
            cols = slice(i * tok, (i + 1) * tok)
            ds.append((scale_ref[g * group + i] * probs[i] * (dprobs[:, cols] - delta[:, cols])).astype(jnp.bfloat16))
        ds_g = jnp.concatenate(ds, axis=1)
        dq_g = transposed_dot(keys_g, ds_g).T
        attn_g = attn_t.T
        for i in range(group):
            attn[:, heads[i]] = attn_g[i * tok : (i + 1) * tok].astype(jnp.bfloat16)
            dq[:, heads[i]] = dq_g[i * tok : (i + 1) * tok]
        dkeys = plain_dot(ds_g, queries_g).reshape(4, tok, HEAD_SIZE)
        dvalues = plain_dot(low_g, grads_g).reshape(4, tok, HEAD_SIZE)
        dkv_own[u, :, lanes] = dkeys[0]
        dkv_own[u, :, value_lanes] = dvalues[0]
        for j in (1, 2, 3):
            dkv_out[u, j - 1, :, lanes] = dkeys[j].astype(jnp.bfloat16)
            dkv_out[u, j - 1, :, value_lanes] = dvalues[j].astype(jnp.bfloat16)
        if g % 2 == 1:
            for j in (3, 2, 1):
                dkv_copies.append(push(dkv_out.at[u, j - 1], dkv_in.at[u, j - 1], dkv_send.at[u, j - 1], dkv_got.at[u, j - 1], along(-j)))
    half_attn = attn.shape[1] // 2
    attn_copy = pair(3, attn.at[:, pl.ds(pl.multiple_of((1 - core) * half_attn, 128), half_attn)], attn_pair.at[core])
    attn_pair[core] = attn[:, pl.ds(pl.multiple_of(core * half_attn, 128), half_attn)]

    def pull(at, g):
        scale = heads_inv[:, at : at + 128]
        x = qk_ref[:, at : at + 128] * scale
        return (scale * (g - x * (half_sums(g * x) / HEAD_SIZE))).astype(jnp.bfloat16)

    for at in range(0, key_start, 128):
        dqkv[:, at : at + 128] = pull(at, dq[:, at : at + 128])

    finals = []
    copies = [None] * parts
    steps = [0] * parts
    done = [None] * parts

    def transfer(part, source):
        partner = chip_partner(orders[part][steps[part]], grid_bits, own_blk, own_grid)[0]
        copies[part] = push(source, recv[part][steps[part]], send_sem.at[part, steps[part]], recv_sem.at[part, steps[part]], partner)

    def begin(members, left, right, extra=None):
        product = transposed_dot(left.reshape(2 * tok, width), right).astype(jnp.bfloat16)
        if extra is not None:
            product = jnp.concatenate([product, extra], axis=1)
        at = 0
        for part in members:
            first[part][...] = product[:, at : at + widths[part]].reshape(first[part].shape)
            at += widths[part]
            mine = chip_partner(orders[part][0], grid_bits, own_blk, own_grid)[1]
            transfer(part, first[part].at[:, 1 - mine])

    def advance(part):
        step = steps[part]
        order = orders[part]
        copies[part].wait()
        held = recv[part][step]
        mine = chip_partner(order[step], grid_bits, own_blk, own_grid)[1]
        left_over = [b for b in range(nb) if b not in order[:step]]
        inner = first[part].shape[2]

        def total(i):
            if step == 0:
                return first[part][i // inner, mine, i % inner].astype(jnp.float32) + held[i // inner, i % inner].astype(jnp.float32)
            return keep[part][step - 1][i] + held[i].astype(jnp.float32)

        steps[part] = step + 1
        if step == nb - 1:
            value = total(0)
            half = value.shape[0] // 2
            final[0, :, offsets[part] : offsets[part] + widths[part]] = value[:half]
            final[1, :, offsets[part] : offsets[part] + widths[part]] = value[half:]
            cols = slice(offsets[part], offsets[part] + widths[part])
            finals.append(pair(6 + part, final.at[1 - core, :, cols], final_recv.at[:, cols]))
            return
        left_over.remove(order[step])
        place_next = 1 << left_over.index(order[step + 1])
        mine_next = chip_partner(order[step + 1], grid_bits, own_blk, own_grid)[1]
        count = 1 << (nb - 2 - step)
        for r in range(count):
            away = r // place_next * (2 * place_next) + (1 - mine_next) * place_next + r % place_next
            send[part][step + 1][r] = total(away).astype(jnp.bfloat16)
        transfer(part, send[part][step + 1])
        for r in range(count):
            here = r // place_next * (2 * place_next) + mine_next * place_next + r % place_next
            keep[part][step][r] = total(here)

    attn_parts, qkv_parts, stem_parts = (0, 1, 2), (3, 4, 5), (6, 7, 8)
    attn_copy.wait()
    grad_copy.wait()
    begin(attn_parts, grad_pair[...], attn_pair[...].reshape(2 * tok, half_attn))

    for copy in dkv_copies:
        copy.wait()
    for u in range(span // 128):
        total_kv = dkv_own[u]
        for j in range(3):
            total_kv = total_kv + dkv_in[u, j].astype(jnp.float32)
        at = key_start + u * 128
        dqkv[:, at : at + 128] = pull(at, total_kv[:, :128])
        dqkv[:, at + span : at + span + 128] = total_kv[:, 128:].astype(jnp.bfloat16)
    half_qkv = dqkv.shape[1] // 2
    dqkv_copy = pair(4, dqkv.at[:, pl.ds(pl.multiple_of((1 - core) * half_qkv, 128), half_qkv)], dqkv_pair.at[core])
    dqkv_pair[core] = dqkv[:, pl.ds(pl.multiple_of(core * half_qkv, 128), half_qkv)]
    for part in attn_parts:
        advance(part)
    d_hidden = rowwise_dot(dqkv[...], wqkv[...])
    normed = normed_ref[...]
    flow = d_hidden * gain_f
    inner_mean = jnp.sum(flow * normed, axis=1, keepdims=True) / width
    d_tokens = grad_ref[...].astype(jnp.float32) + inv_ref[:, :1] * (flow - normed * inner_mean)
    token_pair[core] = d_tokens.astype(jnp.bfloat16)
    token_copy = pair(5, token_pair.at[core], token_pair.at[core])
    gain_term = jnp.sum(d_hidden * normed, axis=0, keepdims=True)
    gain_tile = jnp.broadcast_to(gain_term, (128, width)).T.astype(jnp.bfloat16)
    hidden_copy.wait()
    dqkv_copy.wait()
    begin(qkv_parts, hidden_pair[...], dqkv_pair[...].reshape(2 * tok, half_qkv))
    for part in attn_parts:
        advance(part)
    token_copy.wait()
    tiles_copy.wait()
    begin(stem_parts, token_pair[...], image[pl.ds(pl.multiple_of(core * halo, halo), 2 * tok)], gain_tile)
    for _ in range(nb):
        for part in range(parts):
            if steps[part] < nb:
                advance(part)
    for copy in finals:
        copy.wait()
    half_out, gain_at = out_out.shape[1] // 2, offsets[6] + stem_out.shape[2]
    for source, value in ((core, final.at[core]), (1 - core, final_recv)):
        out_out[:, pl.ds(pl.multiple_of(source * half_out, 128), half_out)] = value[:, : offsets[3]]
        qkv_out[:, pl.ds(pl.multiple_of(source * half_qkv, 128), half_qkv)] = value[:, offsets[3] : offsets[6]]
        stem_out[source] = value[:, offsets[6] : gain_at]
    gain_sum = final[core, :, gain_at:] + final_recv[:, gain_at:]
    square = jnp.concatenate([gain_sum, jnp.zeros((128 - gain_sum.shape[0], 128), jnp.float32)], axis=0).T
    gain_out[...] = square[:1, : gain_out.shape[1]]


def whole_layer(tiles, grad_out, stem_weight, norm_gain, w_qkv, w_out, per_head_scale, positions):
    blk_bits, grid_bits = log2(lax.axis_size("blk")), log2(lax.axis_size("grid")) - 1
    nb = blk_bits + grid_bits
    tok, width = grad_out.shape
    pin = tiles.shape[1]
    qd, span = QUERY_HEADS * HEAD_SIZE, KEY_VALUE_HEADS * HEAD_SIZE
    rows = width >> nb
    half_qkv = w_qkv.shape[1] // 2
    part_widths = []
    for amount in (qd // 2, half_qkv, pin + 128):
        piece = (amount // 3 + 127) // 128 * 128
        part_widths += [piece, piece, amount - 2 * piece]
    offsets = [sum(part_widths[:i]) for i in range(9)]
    grid_first, low = list(range(grid_bits)), list(range(grid_bits, nb))
    turned = [low[i:] + low[:i] for i in (0, 1, 1)]
    orders = [grid_first + rest for rest in turned] + halving_orders(grid_bits, blk_bits) * 2
    firsts, recvs, sends, keeps = [], [], [], []
    for order, w in zip(orders, part_widths):
        inner = 1 << order[0]
        outer = (1 << nb) // (2 * inner)
        firsts.append(pltpu.VMEM((outer, 2, inner, rows, w), jnp.bfloat16))
        recvs.append(pltpu.VMEM((outer, inner, rows, w), jnp.bfloat16))
        for step in range(1, nb):
            shape = (1 << (nb - 1 - step), rows, w)
            recvs.append(pltpu.VMEM(shape, jnp.bfloat16))
            sends.append(pltpu.VMEM(shape, jnp.bfloat16))
            keeps.append(pltpu.VMEM(shape, jnp.float32))
    total = sum(part_widths)
    bf, f32 = jnp.bfloat16, jnp.float32
    buffers = [
        ((2, rows // 2, total), f32),
        ((rows // 2, total), f32),
        (stem_weight.shape, bf),
        (w_qkv.shape, bf),
        (w_out.shape, bf),
        ((2 * tok + TC, pin), bf),
        ((2, tok, width), bf),
        ((2, tok, width), bf),
        ((2, tok, qd // 2), bf),
        ((2, tok, half_qkv), bf),
        ((2, tok, width), bf),
        ((span // 128, 4, tok, 256), bf),
        ((span // 128, 3, tok, 256), bf),
        ((span // 128, tok, 256), f32),
        ((span // 128, 3, tok, 256), bf),
        ((tok, width), f32),
        ((tok, 128), f32),
        ((tok, qd + span), f32),
        ((tok, qd + span), f32),
        ((tok, qd), bf),
        ((tok, qd), bf),
        ((tok, qd), bf),
        ((tok, qd), f32),
        ((tok, w_qkv.shape[1]), bf),
    ]
    dma = pltpu.SemaphoreType.DMA
    halves = span // 128
    vmem = pl.BlockSpec(memory_space=pltpu.VMEM)
    hbm = pl.BlockSpec(memory_space=pl.ANY)
    return pl.pallas_call(
        partial(layer_kernel, (nb, grid_bits, orders, part_widths, offsets)),
        out_shape=[
            jax.ShapeDtypeStruct(shape, f32)
            for shape in ((2, rows // 2, pin), (1, rows // 2), (rows // 2, w_qkv.shape[1]), (rows // 2, qd))
        ],
        in_specs=[pl.BlockSpec(memory_space=pltpu.SMEM), vmem, vmem, hbm, vmem, hbm, hbm, vmem],
        out_specs=[vmem] * 4,
        scratch_shapes=firsts
        + recvs
        + sends
        + keeps
        + [pltpu.VMEM(shape, kind) for shape, kind in buffers]
        + [dma((3,)), dma((15,)), dma((15,)), dma, dma, dma((halves, 4)), dma((halves, 4)), dma((halves, 3)), dma((halves, 3)), dma((9, nb)), dma((9, nb))],
        compiler_params=pltpu.CompilerParams(collective_id=0, has_side_effects=True, vmem_limit_bytes=63000000),
    )(per_head_scale, tiles, grad_out, stem_weight, norm_gain, w_qkv, w_out, positions.reshape(-1, tok))


def shards(patches, stem_weight, norm_gain, w_qkv, w_out, per_head_scale, positions, d_out):
    tiles = patches[0]
    grad_out = d_out[0]
    chips = lax.axis_size("blk") * lax.axis_size("grid") // 2
    if (grad_out.shape[1] // chips) % 16 == 0:
        d_stem, d_gain, d_qkv, d_out_t = whole_layer(
            tiles, grad_out, stem_weight, norm_gain, w_qkv, w_out, per_head_scale, positions
        )
        return (d_stem.transpose(0, 2, 1), d_gain.reshape(-1), d_qkv, d_out_t.T)
    token_rows = tiles.shape[0]
    group_factor = QUERY_HEADS // KEY_VALUE_HEADS
    query_span_width = QUERY_HEADS * HEAD_SIZE
    key_span_width = KEY_VALUE_HEADS * HEAD_SIZE
    arrived = shifted(tiles[:TC], "grid", -1)
    below = jnp.concatenate([tiles[TC:], arrived], axis=0)
    stem = jnp.dot(tiles, stem_weight[0], preferred_element_type=jnp.float32)
    stem = stem + jnp.dot(below, stem_weight[1], preferred_element_type=jnp.float32)
    token_f = lax.optimization_barrier(stem.astype(jnp.bfloat16)).astype(jnp.float32)
    gain_f = norm_gain.astype(jnp.float32)
    normed = row_norm(token_f)
    hidden = (normed * gain_f).astype(jnp.bfloat16)
    query_key_value = jnp.dot(hidden, w_qkv, preferred_element_type=jnp.float32)
    query = query_key_value[:, :query_span_width].reshape(token_rows, QUERY_HEADS, HEAD_SIZE)
    key = query_key_value[:, query_span_width : query_span_width + key_span_width].reshape(
        token_rows, KEY_VALUE_HEADS, HEAD_SIZE
    )
    query_normalized = head_norm(query).astype(jnp.bfloat16)
    key_n = head_norm(key).astype(jnp.bfloat16).reshape(token_rows, key_span_width)
    value = query_key_value[:, query_span_width + key_span_width :].astype(jnp.bfloat16)
    attention_gradient = jnp.dot(grad_out, w_out.T, preferred_element_type=jnp.float32).astype(
        jnp.bfloat16
    )
    kv_own = jnp.concatenate([key_n, value], axis=1)
    blk_count = lax.axis_size("blk")
    own_index = lax.axis_index("blk")
    blocks = [kv_own]
    for offset in range(1, 4):
        blocks.append(passed_along(kv_own, "blk", offset))
    causal_window = jnp.concatenate(blocks, axis=0)
    key_pos = jnp.concatenate(
        [
            lax.dynamic_slice_in_dim(
                positions, (own_index - offset) % blk_count * token_rows, token_rows
            )
            for offset in range(4)
        ]
    )
    query_pos = lax.dynamic_slice_in_dim(positions, own_index * token_rows, token_rows)
    visible = (key_pos[None, :] <= query_pos[:, None])[None]
    every_key = causal_window.shape[0]
    query_cube = query_normalized.reshape(token_rows, KEY_VALUE_HEADS, group_factor, HEAD_SIZE)
    gradient_cube = attention_gradient.reshape(token_rows, KEY_VALUE_HEADS, group_factor, HEAD_SIZE)
    key_cube = causal_window[:, :key_span_width].reshape(every_key, KEY_VALUE_HEADS, HEAD_SIZE)
    value_cube = causal_window[:, key_span_width:].reshape(every_key, KEY_VALUE_HEADS, HEAD_SIZE)
    score_scales = per_head_scale.reshape(KEY_VALUE_HEADS, group_factor)
    prob_list = []
    low_list = []
    attn_list = []
    for query_head_group in range(KEY_VALUE_HEADS):
        scale_col = score_scales[query_head_group][:, None, None]
        attention_scores = (
            jnp.einsum(
                "trd,sd->rts",
                query_cube[:, query_head_group],
                key_cube[:, query_head_group],
                preferred_element_type=jnp.float32,
            )
            * scale_col
        )
        attention_scores = jnp.where(visible, attention_scores, -1e30)
        top = jnp.max(attention_scores, axis=-1, keepdims=True)
        weights = jnp.where(visible, jnp.exp(attention_scores - top), 0.0)
        probs = weights / jnp.sum(weights, axis=-1, keepdims=True)
        probability_narrow = probs.astype(jnp.bfloat16)
        prob_list.append(probs)
        low_list.append(probability_narrow)
        attn_list.append(
            jnp.einsum(
                "rts,sd->trd",
                probability_narrow,
                value_cube[:, query_head_group],
                preferred_element_type=jnp.float32,
            )
        )
    attention_output = (
        jnp.stack(attn_list, axis=1).reshape(token_rows, query_span_width).astype(jnp.bfloat16)
    )
    dquery_list = []
    dkey_list = []
    dvalue_list = []
    for query_head_group in range(KEY_VALUE_HEADS):
        scale_col = score_scales[query_head_group][:, None, None]
        grad_group = gradient_cube[:, query_head_group]
        softmax_delta = jnp.sum(
            grad_group.astype(jnp.float32) * attn_list[query_head_group], axis=-1
        )
        probability_gradient = jnp.einsum(
            "trd,sd->rts",
            grad_group,
            value_cube[:, query_head_group],
            preferred_element_type=jnp.float32,
        )
        score_gradient = (
            scale_col
            * prob_list[query_head_group]
            * (probability_gradient - softmax_delta.T[:, :, None])
        ).astype(jnp.bfloat16)
        dquery_list.append(
            jnp.einsum(
                "rts,sd->trd",
                score_gradient,
                key_cube[:, query_head_group],
                preferred_element_type=jnp.float32,
            )
        )
        dkey_list.append(
            jnp.einsum(
                "rts,trd->sd",
                score_gradient,
                query_cube[:, query_head_group],
                preferred_element_type=jnp.float32,
            )
        )
        dvalue_list.append(
            jnp.einsum(
                "rts,trd->sd",
                low_list[query_head_group],
                grad_group,
                preferred_element_type=jnp.float32,
            )
        )
    query_gradient = jnp.stack(dquery_list, axis=1).reshape(token_rows, QUERY_HEADS, HEAD_SIZE)
    dkey_all = jnp.stack(dkey_list, axis=1).reshape(every_key, key_span_width)
    dvalue_all = jnp.stack(dvalue_list, axis=1).reshape(every_key, key_span_width)
    partial_terms = jnp.concatenate([dkey_all, dvalue_all], axis=1)
    pieces = [partial_terms[offset * token_rows : (offset + 1) * token_rows] for offset in range(4)]
    carried_state = pieces[0]
    for offset in (1, 2, 3):
        carried_state = carried_state + passed_along(pieces[offset], "blk", -offset)
    pull_query = jax.vjp(head_norm, query)[1]
    gather_key = jax.vjp(head_norm, key)[1]
    dq_full = pull_query(query_gradient)[0].reshape(token_rows, query_span_width)
    key_gradient_whole = gather_key(
        carried_state[:, :key_span_width].reshape(token_rows, KEY_VALUE_HEADS, HEAD_SIZE)
    )[0].reshape(token_rows, key_span_width)
    d_qkv = jnp.concatenate(
        [dq_full, key_gradient_whole, carried_state[:, key_span_width:]], axis=1
    ).astype(jnp.bfloat16)
    d_hidden = jnp.dot(d_qkv, w_qkv.T, preferred_element_type=jnp.float32)
    gain_term = jnp.sum(d_hidden * normed, axis=0)
    pull_tokens = jax.vjp(row_norm, token_f)[1]
    d_tokens = (grad_out.astype(jnp.float32) + pull_tokens(d_hidden * gain_f)[0]).astype(
        jnp.bfloat16
    )
    stem_term = jnp.stack(
        [
            jnp.dot(tiles.T, d_tokens, preferred_element_type=jnp.float32),
            jnp.dot(below.T, d_tokens, preferred_element_type=jnp.float32),
        ]
    )
    qkv_term = jnp.dot(hidden.T, d_qkv, preferred_element_type=jnp.float32)
    out_term = jnp.dot(attention_output.T, grad_out, preferred_element_type=jnp.float32)
    d_stem_weight = lax.psum_scatter(stem_term, ("blk", "grid"), scatter_dimension=2, tiled=True)
    d_norm_gain = lax.psum_scatter(gain_term, ("blk", "grid"), scatter_dimension=0, tiled=True)
    d_w_qkv = lax.psum_scatter(qkv_term, ("blk", "grid"), scatter_dimension=0, tiled=True)
    d_w_out = lax.psum_scatter(out_term, ("blk", "grid"), scatter_dimension=1, tiled=True)
    return (d_stem_weight, d_norm_gain, d_w_qkv, d_w_out)


def solution(mesh):
    placed = (P("grid", "blk", None), P(), P(), P(), P(), P(), P(), P("grid", "blk", None))
    return jax.shard_map(
        shards,
        mesh=mesh,
        in_specs=placed,
        out_specs=(
            P(None, None, ("blk", "grid")),
            P(("blk", "grid")),
            P(("blk", "grid"), None),
            P(None, ("blk", "grid")),
        ),
        check_vma=False,
    )
```

```python
from functools import partial

import jax
import jax.numpy as jnp
from jax import lax
from jax.experimental import pallas as pl
from jax.experimental.pallas import tpu as pltpu
from jax.sharding import PartitionSpec as P

QUERY_HEADS = 12
KEY_VALUE_HEADS = 4
HEAD_SIZE = 64
TC = 16


def shifted(x, axis, by):
    peers = lax.axis_size(axis)
    pairs = [(i, i + by) for i in range(peers) if 0 <= i + by < peers]
    return lax.ppermute(x, axis, pairs)


def passed_along(x, axis, by):
    peers = lax.axis_size(axis)
    return lax.ppermute(x, axis, [(i, (i + by) % peers) for i in range(peers)])


def row_norm(values):
    return values * lax.rsqrt(jnp.mean(values * values, axis=-1, keepdims=True) + 1e-05)


def head_norm(values):
    return values * lax.rsqrt(jnp.mean(values * values, axis=-1, keepdims=True) + 1e-06)


def log2(n):
    return n.bit_length() - 1


def halving_orders(grid_bits, blk_bits):
    y = list(range(grid_bits))
    low = list(range(grid_bits, grid_bits + blk_bits))
    rest = low[1:]
    return [y + rest[:1] + rest[1:] + low[:1], low[:1] + y + rest, rest[:1] + low[:1] + y + rest[1:]]


def chip_partner(bit, grid_bits, own_blk, own_grid):
    if bit < grid_bits:
        step = 2 << bit
        mine = own_grid // step % 2
        return {"blk": own_blk, "grid": own_grid + (1 - 2 * mine) * step}, mine
    step = 1 << (bit - grid_bits)
    mine = own_blk // step % 2
    return {"blk": own_blk + (1 - 2 * mine) * step, "grid": own_grid}, mine


def transposed_dot(a, b):
    return lax.dot_general(a, b, (((0,), (0,)), ((), ())), preferred_element_type=jnp.float32)


def rowwise_dot(a, b):
    return lax.dot_general(a, b, (((1,), (1,)), ((), ())), preferred_element_type=jnp.float32)


def plain_dot(a, b):
    return jnp.dot(a, b, preferred_element_type=jnp.float32)


def half_sums(x):
    low = lax.broadcasted_iota(jnp.int32, x.shape, 1) < HEAD_SIZE
    first = jnp.sum(jnp.where(low, x, 0.0), axis=1, keepdims=True)
    second = jnp.sum(jnp.where(low, 0.0, x), axis=1, keepdims=True)
    return jnp.where(low, first, second)


def layer_kernel(plan, *refs):
    nb, grid_bits, orders, widths, offsets = plan
    (scale_ref, tiles_ref, grad_ref, stem_hbm, gain_ref, wqkv_hbm, wout_hbm, pos_ref, result_ref) = refs[:9]
    scratch = list(refs[9:])
    parts = len(widths)
    first = [scratch.pop(0) for _ in range(parts)]
    recv = [[scratch.pop(0) for _ in range(nb)] for _ in range(parts)]
    send = [[None] + [scratch.pop(0) for _ in range(nb - 1)] for _ in range(parts)]
    keep = [[scratch.pop(0) for _ in range(nb - 1)] for _ in range(parts)]
    (final, final_recv, stem_w, wqkv, wout, image, grad_pair, hidden_pair, attn_pair, dqkv_pair, token_pair,
     kv, dkv_out, dkv_own, dkv_in, normed_ref, inv_ref, qk_ref, heads_inv, qn, da, attn, dq, dqkv,
     load_sem, pair_send, pair_got, halo_send, halo_got, kv_send, kv_got, dkv_send, dkv_got, send_sem, recv_sem) = scratch
    tok, width = grad_ref.shape
    halo = image.shape[0] - 2 * tok
    span = kv.shape[0] * 128
    group = QUERY_HEADS // KEY_VALUE_HEADS
    own_blk = lax.axis_index("blk")
    own_grid = lax.axis_index("grid")
    blk_count = lax.axis_size("blk")
    grid_count = lax.axis_size("grid")
    core = own_grid % 2
    other_core = {"blk": own_blk, "grid": own_grid + 1 - 2 * core}
    above = {"blk": own_blk, "grid": (own_grid + grid_count - 1) % grid_count}
    under = {"blk": own_blk, "grid": (own_grid + 1) % grid_count}

    def along(offset):
        return {"blk": (own_blk + offset + blk_count) % blk_count, "grid": own_grid}

    loads = [
        pltpu.make_async_copy(stem_hbm, stem_w, load_sem.at[0]),
        pltpu.make_async_copy(wqkv_hbm, wqkv, load_sem.at[1]),
        pltpu.make_async_copy(wout_hbm, wout, load_sem.at[2]),
    ]
    for load in loads:
        load.start()

    barrier = pltpu.get_barrier_semaphore()
    peers = [chip_partner(bit, grid_bits, own_blk, own_grid)[0] for bit in range(nb)]
    peers += [other_core, above, under] + [along(j) for j in (1, 2, 3, -1, -2, -3)]
    for peer in peers:
        pl.semaphore_signal(barrier, inc=1, device_id=peer, device_id_type=pl.DeviceIdType.MESH)
    pl.semaphore_wait(barrier, len(peers))

    def push(source, target, sems, got, device):
        copy = pltpu.make_async_remote_copy(
            src_ref=source, dst_ref=target, send_sem=sems, recv_sem=got, device_id=device, device_id_type=pl.DeviceIdType.MESH
        )
        copy.start()
        return copy

    def pair(which, source, target):
        return push(source, target, pair_send.at[which], pair_got.at[which], other_core)

    own_rows = pl.ds(pl.multiple_of(core * tok, tok), tok)
    halo_copy = push(tiles_ref.at[:halo], image.at[2 * tok :], halo_send, halo_got, above)

    loads[0].wait()
    stem = plain_dot(tiles_ref[...], stem_w[0])
    halo_copy.wait()

    @pl.when(own_grid == grid_count - 1)
    def _():
        image[2 * tok :] = jnp.zeros((halo, image.shape[1]), image.dtype)

    below = jnp.concatenate([tiles_ref[halo:], image[2 * tok :]], axis=0)
    stem = stem + plain_dot(below, stem_w[1])
    token_f = stem.astype(jnp.bfloat16).astype(jnp.float32)
    inv = lax.rsqrt(jnp.sum(token_f * token_f, axis=1, keepdims=True) / width + 1e-05)
    normed = token_f * inv
    normed_ref[...] = normed
    inv_ref[...] = jnp.broadcast_to(inv, inv_ref.shape)
    gain_f = gain_ref[...].astype(jnp.float32).reshape(1, width)
    hidden = (normed * gain_f).astype(jnp.bfloat16)
    hidden_pair[core] = hidden
    loads[1].wait()
    key_start = QUERY_HEADS * HEAD_SIZE
    value_start = key_start + span

    def normalize(x):
        scale = lax.rsqrt(half_sums(x * x) / HEAD_SIZE + 1e-06)
        return scale, (x * scale).astype(jnp.bfloat16)

    keys = plain_dot(hidden, wqkv[:, key_start:])
    kv_copies = []
    for u in range(span // 128):
        at = u * 128
        heads_inv[:, key_start + at : key_start + at + 128], kv[u, 0, :, :128] = normalize(keys[:, at : at + 128])
        kv[u, 0, :, 128:] = keys[:, span + at : span + at + 128].astype(jnp.bfloat16)
        kv_copies.append([push(kv.at[u, 0], kv.at[u, j], kv_send.at[u, j], kv_got.at[u, j], along(j)) for j in (3, 2, 1)])
    qk_ref[:, key_start:] = keys[:, :span]
    tiles_copy = pair(0, tiles_ref, image.at[own_rows])
    grad_copy = pair(1, grad_ref, grad_pair.at[core])
    hidden_copy = pair(2, hidden_pair.at[core], hidden_pair.at[core])
    image[own_rows] = tiles_ref[...]
    grad_pair[core] = grad_ref[...]
    queries = plain_dot(hidden, wqkv[:, :key_start])
    qk_ref[:, :key_start] = queries
    for at in range(0, key_start, 128):
        heads_inv[:, at : at + 128], qn[:, at : at + 128] = normalize(queries[:, at : at + 128])
    loads[2].wait()
    da[...] = rowwise_dot(grad_ref[...], wout[...]).astype(jnp.bfloat16)

    query_pos = pos_ref[pl.ds(own_blk, 1), :]
    seen = []
    for j in range(4):
        key_pos = pos_ref[pl.ds((own_blk + blk_count - j) % blk_count, 1), :]
        column = jnp.broadcast_to(key_pos, (tok, tok)).T
        seen.append(column <= query_pos)
    visible = jnp.concatenate([jnp.where(x, 1.0, 0.0) for x in seen], axis=0) > 0.5
    dkv_copies = []
    for g in range(KEY_VALUE_HEADS):
        u, low_lane = g // 2, g % 2 * HEAD_SIZE
        lanes = slice(low_lane, low_lane + HEAD_SIZE)
        value_lanes = slice(128 + low_lane, 128 + low_lane + HEAD_SIZE)
        if g % 2 == 0:
            for copy in kv_copies[u]:
                copy.wait()
        keys_g = kv[u, :, :, lanes].reshape(4 * tok, HEAD_SIZE)
        values_g = kv[u, :, :, value_lanes].reshape(4 * tok, HEAD_SIZE)
        heads = [slice((g * group + i) * HEAD_SIZE, (g * group + i + 1) * HEAD_SIZE) for i in range(group)]
        queries_g = jnp.concatenate([qn[:, h] for h in heads], axis=0)
        grads_g = jnp.concatenate([da[:, h] for h in heads], axis=0)
        scores = rowwise_dot(keys_g, queries_g)
        dprobs = rowwise_dot(values_g, grads_g)
        probs, low = [], []
        for i in range(group):
            s = jnp.where(visible, scores[:, i * tok : (i + 1) * tok] * scale_ref[g * group + i], -1e30)
            weights = jnp.where(visible, jnp.exp(s - jnp.max(s, axis=0, keepdims=True)), 0.0)
            p = weights * (1.0 / jnp.sum(weights, axis=0, keepdims=True))
            probs.append(p)
            low.append(p.astype(jnp.bfloat16))
        low_g = jnp.concatenate(low, axis=1)
        attn_t = transposed_dot(values_g, low_g)
        delta = jnp.sum(grads_g.astype(jnp.float32).T * attn_t, axis=0, keepdims=True)
        ds = []
        for i in range(group):
            cols = slice(i * tok, (i + 1) * tok)
            ds.append((scale_ref[g * group + i] * probs[i] * (dprobs[:, cols] - delta[:, cols])).astype(jnp.bfloat16))
        ds_g = jnp.concatenate(ds, axis=1)
        dq_g = transposed_dot(keys_g, ds_g).T
        attn_g = attn_t.T
        for i in range(group):
            attn[:, heads[i]] = attn_g[i * tok : (i + 1) * tok].astype(jnp.bfloat16)
            dq[:, heads[i]] = dq_g[i * tok : (i + 1) * tok]
        dkeys = plain_dot(ds_g, queries_g).reshape(4, tok, HEAD_SIZE)
        dvalues = plain_dot(low_g, grads_g).reshape(4, tok, HEAD_SIZE)
        dkv_own[u, :, lanes] = dkeys[0]
        dkv_own[u, :, value_lanes] = dvalues[0]
        for j in (1, 2, 3):
            dkv_out[u, j - 1, :, lanes] = dkeys[j].astype(jnp.bfloat16)
            dkv_out[u, j - 1, :, value_lanes] = dvalues[j].astype(jnp.bfloat16)
        if g % 2 == 1:
            for j in (3, 2, 1):
                dkv_copies.append(push(dkv_out.at[u, j - 1], dkv_in.at[u, j - 1], dkv_send.at[u, j - 1], dkv_got.at[u, j - 1], along(-j)))
    half_attn = attn.shape[1] // 2
    attn_copy = pair(3, attn.at[:, pl.ds(pl.multiple_of((1 - core) * half_attn, 128), half_attn)], attn_pair.at[core])
    attn_pair[core] = attn[:, pl.ds(pl.multiple_of(core * half_attn, 128), half_attn)]

    def pull(at, g):
        scale = heads_inv[:, at : at + 128]
        x = qk_ref[:, at : at + 128] * scale
        return (scale * (g - x * (half_sums(g * x) / HEAD_SIZE))).astype(jnp.bfloat16)

    for at in range(0, key_start, 128):
        dqkv[:, at : at + 128] = pull(at, dq[:, at : at + 128])

    finals = []
    copies = [None] * parts
    steps = [0] * parts
    done = [None] * parts

    def transfer(part, source):
        partner = chip_partner(orders[part][steps[part]], grid_bits, own_blk, own_grid)[0]
        copies[part] = push(source, recv[part][steps[part]], send_sem.at[part, steps[part]], recv_sem.at[part, steps[part]], partner)

    def begin(members, left, right, extra=None):
        product = transposed_dot(left.reshape(2 * tok, width), right).astype(jnp.bfloat16)
        if extra is not None:
            product = jnp.concatenate([product, extra], axis=1)
        at = 0
        for part in members:
            first[part][...] = product[:, at : at + widths[part]].reshape(first[part].shape)
            at += widths[part]
            mine = chip_partner(orders[part][0], grid_bits, own_blk, own_grid)[1]
            transfer(part, first[part].at[:, 1 - mine])

    def advance(part):
        step = steps[part]
        order = orders[part]
        copies[part].wait()
        held = recv[part][step]
        mine = chip_partner(order[step], grid_bits, own_blk, own_grid)[1]
        left_over = [b for b in range(nb) if b not in order[:step]]
        inner = first[part].shape[2]

        def total(i):
            if step == 0:
                return first[part][i // inner, mine, i % inner].astype(jnp.float32) + held[i // inner, i % inner].astype(jnp.float32)
            return keep[part][step - 1][i] + held[i].astype(jnp.float32)

        steps[part] = step + 1
        if step == nb - 1:
            value = total(0)
            half = value.shape[0] // 2
            final[0, :, offsets[part] : offsets[part] + widths[part]] = value[:half]
            final[1, :, offsets[part] : offsets[part] + widths[part]] = value[half:]
            cols = slice(offsets[part], offsets[part] + widths[part])
            finals.append(pair(6 + part, final.at[1 - core, :, cols], final_recv.at[:, cols]))
            return
        left_over.remove(order[step])
        place_next = 1 << left_over.index(order[step + 1])
        mine_next = chip_partner(order[step + 1], grid_bits, own_blk, own_grid)[1]
        count = 1 << (nb - 2 - step)
        for r in range(count):
            away = r // place_next * (2 * place_next) + (1 - mine_next) * place_next + r % place_next
            send[part][step + 1][r] = total(away).astype(jnp.bfloat16)
        transfer(part, send[part][step + 1])
        for r in range(count):
            here = r // place_next * (2 * place_next) + mine_next * place_next + r % place_next
            keep[part][step][r] = total(here)

    attn_parts, qkv_parts, stem_parts = (0, 1, 2), (3, 4, 5), (6, 7, 8)
    attn_copy.wait()
    grad_copy.wait()
    begin(attn_parts, grad_pair[...], attn_pair[...].reshape(2 * tok, half_attn))

    for copy in dkv_copies:
        copy.wait()
    for u in range(span // 128):
        total_kv = dkv_own[u]
        for j in range(3):
            total_kv = total_kv + dkv_in[u, j].astype(jnp.float32)
        at = key_start + u * 128
        dqkv[:, at : at + 128] = pull(at, total_kv[:, :128])
        dqkv[:, at + span : at + span + 128] = total_kv[:, 128:].astype(jnp.bfloat16)
    half_qkv = dqkv.shape[1] // 2
    dqkv_copy = pair(4, dqkv.at[:, pl.ds(pl.multiple_of((1 - core) * half_qkv, 128), half_qkv)], dqkv_pair.at[core])
    dqkv_pair[core] = dqkv[:, pl.ds(pl.multiple_of(core * half_qkv, 128), half_qkv)]
    d_hidden = rowwise_dot(dqkv[...], wqkv[...])
    normed = normed_ref[...]
    flow = d_hidden * gain_f
    inner_mean = jnp.sum(flow * normed, axis=1, keepdims=True) / width
    d_tokens = grad_ref[...].astype(jnp.float32) + inv_ref[:, :1] * (flow - normed * inner_mean)
    token_pair[core] = d_tokens.astype(jnp.bfloat16)
    token_copy = pair(5, token_pair.at[core], token_pair.at[core])
    gain_term = jnp.sum(d_hidden * normed, axis=0, keepdims=True)
    gain_tile = jnp.broadcast_to(gain_term, (128, width)).T.astype(jnp.bfloat16)
    hidden_copy.wait()
    dqkv_copy.wait()
    begin(qkv_parts, hidden_pair[...], dqkv_pair[...].reshape(2 * tok, half_qkv))
    token_copy.wait()
    tiles_copy.wait()
    begin(stem_parts, token_pair[...], image[pl.ds(pl.multiple_of(core * halo, halo), 2 * tok)], gain_tile)
    for _ in range(nb):
        for part in range(parts):
            if steps[part] < nb:
                advance(part)
    for copy in finals:
        copy.wait()
    result_ref[core] = final[core]
    result_ref[1 - core] = final_recv[...]


def unpack_kernel(offsets, result_ref, stem_out, gain_out, qkv_out, out_out):
    half_out, half_qkv, gain_at = out_out.shape[1] // 2, qkv_out.shape[1] // 2, offsets[6] + stem_out.shape[2]
    for source in range(2):
        out_out[:, source * half_out : (source + 1) * half_out] = result_ref[source, :, : offsets[3]]
        qkv_out[:, source * half_qkv : (source + 1) * half_qkv] = result_ref[source, :, offsets[3] : offsets[6]]
        stem_out[source] = result_ref[source, :, offsets[6] : gain_at]
    gain_sum = result_ref[0, :, gain_at:] + result_ref[1, :, gain_at:]
    square = jnp.concatenate([gain_sum, jnp.zeros((128 - gain_sum.shape[0], 128), jnp.float32)], axis=0).T
    gain_out[...] = square[:1, : gain_out.shape[1]]


def whole_layer(tiles, grad_out, stem_weight, norm_gain, w_qkv, w_out, per_head_scale, positions):
    blk_bits, grid_bits = log2(lax.axis_size("blk")), log2(lax.axis_size("grid")) - 1
    nb = blk_bits + grid_bits
    tok, width = grad_out.shape
    pin = tiles.shape[1]
    qd, span = QUERY_HEADS * HEAD_SIZE, KEY_VALUE_HEADS * HEAD_SIZE
    rows = width >> nb
    half_qkv = w_qkv.shape[1] // 2
    part_widths = []
    for amount in (qd // 2, half_qkv, pin + 128):
        piece = (amount // 3 + 127) // 128 * 128
        part_widths += [piece, piece, amount - 2 * piece]
    offsets = [sum(part_widths[:i]) for i in range(9)]
    grid_first, low = list(range(grid_bits)), list(range(grid_bits, nb))
    turned = [low[i:] + low[:i] for i in (0, 1, 1)]
    orders = halving_orders(grid_bits, blk_bits) * 3
    firsts, recvs, sends, keeps = [], [], [], []
    for order, w in zip(orders, part_widths):
        inner = 1 << order[0]
        outer = (1 << nb) // (2 * inner)
        firsts.append(pltpu.VMEM((outer, 2, inner, rows, w), jnp.bfloat16))
        recvs.append(pltpu.VMEM((outer, inner, rows, w), jnp.bfloat16))
        for step in range(1, nb):
            shape = (1 << (nb - 1 - step), rows, w)
            recvs.append(pltpu.VMEM(shape, jnp.bfloat16))
            sends.append(pltpu.VMEM(shape, jnp.bfloat16))
            keeps.append(pltpu.VMEM(shape, jnp.float32))
    total = sum(part_widths)
    bf, f32 = jnp.bfloat16, jnp.float32
    buffers = [
        ((2, rows // 2, total), f32),
        ((rows // 2, total), f32),
        (stem_weight.shape, bf),
        (w_qkv.shape, bf),
        (w_out.shape, bf),
        ((2 * tok + TC, pin), bf),
        ((2, tok, width), bf),
        ((2, tok, width), bf),
        ((2, tok, qd // 2), bf),
        ((2, tok, half_qkv), bf),
        ((2, tok, width), bf),
        ((span // 128, 4, tok, 256), bf),
        ((span // 128, 3, tok, 256), bf),
        ((span // 128, tok, 256), f32),
        ((span // 128, 3, tok, 256), bf),
        ((tok, width), f32),
        ((tok, 128), f32),
        ((tok, qd + span), f32),
        ((tok, qd + span), f32),
        ((tok, qd), bf),
        ((tok, qd), bf),
        ((tok, qd), bf),
        ((tok, qd), f32),
        ((tok, w_qkv.shape[1]), bf),
    ]
    dma = pltpu.SemaphoreType.DMA
    halves = span // 128
    vmem = pl.BlockSpec(memory_space=pltpu.VMEM)
    hbm = pl.BlockSpec(memory_space=pl.ANY)
    result = pl.pallas_call(
        partial(layer_kernel, (nb, grid_bits, orders, part_widths, offsets)),
        out_shape=jax.ShapeDtypeStruct((2, rows // 2, total), f32),
        in_specs=[pl.BlockSpec(memory_space=pltpu.SMEM), vmem, vmem, hbm, vmem, hbm, hbm, vmem],
        out_specs=vmem,
        scratch_shapes=firsts
        + recvs
        + sends
        + keeps
        + [pltpu.VMEM(shape, kind) for shape, kind in buffers]
        + [dma((3,)), dma((15,)), dma((15,)), dma, dma, dma((halves, 4)), dma((halves, 4)), dma((halves, 3)), dma((halves, 3)), dma((9, nb)), dma((9, nb))],
        compiler_params=pltpu.CompilerParams(collective_id=0, has_side_effects=True, vmem_limit_bytes=63000000),
    )(per_head_scale, tiles, grad_out, stem_weight, norm_gain, w_qkv, w_out, positions.reshape(-1, tok))
    return pl.pallas_call(
        partial(unpack_kernel, offsets),
        out_shape=[
            jax.ShapeDtypeStruct(shape, f32)
            for shape in ((2, rows // 2, pin), (1, rows // 2), (rows // 2, w_qkv.shape[1]), (rows // 2, qd))
        ],
        in_specs=[vmem],
        out_specs=[vmem] * 4,
    )(result)


def shards(patches, stem_weight, norm_gain, w_qkv, w_out, per_head_scale, positions, d_out):
    tiles = patches[0]
    grad_out = d_out[0]
    chips = lax.axis_size("blk") * lax.axis_size("grid") // 2
    if (grad_out.shape[1] // chips) % 16 == 0:
        d_stem, d_gain, d_qkv, d_out_t = whole_layer(
            tiles, grad_out, stem_weight, norm_gain, w_qkv, w_out, per_head_scale, positions
        )
        return (d_stem.transpose(0, 2, 1), d_gain.reshape(-1), d_qkv, d_out_t.T)
    token_rows = tiles.shape[0]
    group_factor = QUERY_HEADS // KEY_VALUE_HEADS
    query_span_width = QUERY_HEADS * HEAD_SIZE
    key_span_width = KEY_VALUE_HEADS * HEAD_SIZE
    arrived = shifted(tiles[:TC], "grid", -1)
    below = jnp.concatenate([tiles[TC:], arrived], axis=0)
    stem = jnp.dot(tiles, stem_weight[0], preferred_element_type=jnp.float32)
    stem = stem + jnp.dot(below, stem_weight[1], preferred_element_type=jnp.float32)
    token_f = lax.optimization_barrier(stem.astype(jnp.bfloat16)).astype(jnp.float32)
    gain_f = norm_gain.astype(jnp.float32)
    normed = row_norm(token_f)
    hidden = (normed * gain_f).astype(jnp.bfloat16)
    query_key_value = jnp.dot(hidden, w_qkv, preferred_element_type=jnp.float32)
    query = query_key_value[:, :query_span_width].reshape(token_rows, QUERY_HEADS, HEAD_SIZE)
    key = query_key_value[:, query_span_width : query_span_width + key_span_width].reshape(
        token_rows, KEY_VALUE_HEADS, HEAD_SIZE
    )
    query_normalized = head_norm(query).astype(jnp.bfloat16)
    key_n = head_norm(key).astype(jnp.bfloat16).reshape(token_rows, key_span_width)
    value = query_key_value[:, query_span_width + key_span_width :].astype(jnp.bfloat16)
    attention_gradient = jnp.dot(grad_out, w_out.T, preferred_element_type=jnp.float32).astype(
        jnp.bfloat16
    )
    kv_own = jnp.concatenate([key_n, value], axis=1)
    blk_count = lax.axis_size("blk")
    own_index = lax.axis_index("blk")
    blocks = [kv_own]
    for offset in range(1, 4):
        blocks.append(passed_along(kv_own, "blk", offset))
    causal_window = jnp.concatenate(blocks, axis=0)
    key_pos = jnp.concatenate(
        [
            lax.dynamic_slice_in_dim(
                positions, (own_index - offset) % blk_count * token_rows, token_rows
            )
            for offset in range(4)
        ]
    )
    query_pos = lax.dynamic_slice_in_dim(positions, own_index * token_rows, token_rows)
    visible = (key_pos[None, :] <= query_pos[:, None])[None]
    every_key = causal_window.shape[0]
    query_cube = query_normalized.reshape(token_rows, KEY_VALUE_HEADS, group_factor, HEAD_SIZE)
    gradient_cube = attention_gradient.reshape(token_rows, KEY_VALUE_HEADS, group_factor, HEAD_SIZE)
    key_cube = causal_window[:, :key_span_width].reshape(every_key, KEY_VALUE_HEADS, HEAD_SIZE)
    value_cube = causal_window[:, key_span_width:].reshape(every_key, KEY_VALUE_HEADS, HEAD_SIZE)
    score_scales = per_head_scale.reshape(KEY_VALUE_HEADS, group_factor)
    prob_list = []
    low_list = []
    attn_list = []
    for query_head_group in range(KEY_VALUE_HEADS):
        scale_col = score_scales[query_head_group][:, None, None]
        attention_scores = (
            jnp.einsum(
                "trd,sd->rts",
                query_cube[:, query_head_group],
                key_cube[:, query_head_group],
                preferred_element_type=jnp.float32,
            )
            * scale_col
        )
        attention_scores = jnp.where(visible, attention_scores, -1e30)
        top = jnp.max(attention_scores, axis=-1, keepdims=True)
        weights = jnp.where(visible, jnp.exp(attention_scores - top), 0.0)
        probs = weights / jnp.sum(weights, axis=-1, keepdims=True)
        probability_narrow = probs.astype(jnp.bfloat16)
        prob_list.append(probs)
        low_list.append(probability_narrow)
        attn_list.append(
            jnp.einsum(
                "rts,sd->trd",
                probability_narrow,
                value_cube[:, query_head_group],
                preferred_element_type=jnp.float32,
            )
        )
    attention_output = (
        jnp.stack(attn_list, axis=1).reshape(token_rows, query_span_width).astype(jnp.bfloat16)
    )
    dquery_list = []
    dkey_list = []
    dvalue_list = []
    for query_head_group in range(KEY_VALUE_HEADS):
        scale_col = score_scales[query_head_group][:, None, None]
        grad_group = gradient_cube[:, query_head_group]
        softmax_delta = jnp.sum(
            grad_group.astype(jnp.float32) * attn_list[query_head_group], axis=-1
        )
        probability_gradient = jnp.einsum(
            "trd,sd->rts",
            grad_group,
            value_cube[:, query_head_group],
            preferred_element_type=jnp.float32,
        )
        score_gradient = (
            scale_col
            * prob_list[query_head_group]
            * (probability_gradient - softmax_delta.T[:, :, None])
        ).astype(jnp.bfloat16)
        dquery_list.append(
            jnp.einsum(
                "rts,sd->trd",
                score_gradient,
                key_cube[:, query_head_group],
                preferred_element_type=jnp.float32,
            )
        )
        dkey_list.append(
            jnp.einsum(
                "rts,trd->sd",
                score_gradient,
                query_cube[:, query_head_group],
                preferred_element_type=jnp.float32,
            )
        )
        dvalue_list.append(
            jnp.einsum(
                "rts,trd->sd",
                low_list[query_head_group],
                grad_group,
                preferred_element_type=jnp.float32,
            )
        )
    query_gradient = jnp.stack(dquery_list, axis=1).reshape(token_rows, QUERY_HEADS, HEAD_SIZE)
    dkey_all = jnp.stack(dkey_list, axis=1).reshape(every_key, key_span_width)
    dvalue_all = jnp.stack(dvalue_list, axis=1).reshape(every_key, key_span_width)
    partial_terms = jnp.concatenate([dkey_all, dvalue_all], axis=1)
    pieces = [partial_terms[offset * token_rows : (offset + 1) * token_rows] for offset in range(4)]
    carried_state = pieces[0]
    for offset in (1, 2, 3):
        carried_state = carried_state + passed_along(pieces[offset], "blk", -offset)
    pull_query = jax.vjp(head_norm, query)[1]
    gather_key = jax.vjp(head_norm, key)[1]
    dq_full = pull_query(query_gradient)[0].reshape(token_rows, query_span_width)
    key_gradient_whole = gather_key(
        carried_state[:, :key_span_width].reshape(token_rows, KEY_VALUE_HEADS, HEAD_SIZE)
    )[0].reshape(token_rows, key_span_width)
    d_qkv = jnp.concatenate(
        [dq_full, key_gradient_whole, carried_state[:, key_span_width:]], axis=1
    ).astype(jnp.bfloat16)
    d_hidden = jnp.dot(d_qkv, w_qkv.T, preferred_element_type=jnp.float32)
    gain_term = jnp.sum(d_hidden * normed, axis=0)
    pull_tokens = jax.vjp(row_norm, token_f)[1]
    d_tokens = (grad_out.astype(jnp.float32) + pull_tokens(d_hidden * gain_f)[0]).astype(
        jnp.bfloat16
    )
    stem_term = jnp.stack(
        [
            jnp.dot(tiles.T, d_tokens, preferred_element_type=jnp.float32),
            jnp.dot(below.T, d_tokens, preferred_element_type=jnp.float32),
        ]
    )
    qkv_term = jnp.dot(hidden.T, d_qkv, preferred_element_type=jnp.float32)
    out_term = jnp.dot(attention_output.T, grad_out, preferred_element_type=jnp.float32)
    d_stem_weight = lax.psum_scatter(stem_term, ("blk", "grid"), scatter_dimension=2, tiled=True)
    d_norm_gain = lax.psum_scatter(gain_term, ("blk", "grid"), scatter_dimension=0, tiled=True)
    d_w_qkv = lax.psum_scatter(qkv_term, ("blk", "grid"), scatter_dimension=0, tiled=True)
    d_w_out = lax.psum_scatter(out_term, ("blk", "grid"), scatter_dimension=1, tiled=True)
    return (d_stem_weight, d_norm_gain, d_w_qkv, d_w_out)


def solution(mesh):
    placed = (P("grid", "blk", None), P(), P(), P(), P(), P(), P(), P("grid", "blk", None))
    return jax.shard_map(
        shards,
        mesh=mesh,
        in_specs=placed,
        out_specs=(
            P(None, None, ("blk", "grid")),
            P(("blk", "grid")),
            P(("blk", "grid"), None),
            P(None, ("blk", "grid")),
        ),
        check_vma=False,
    )
```
